32 devices in a mesh: dp: 16 (over z, x, core), mp: 2 (over y).
Axes of the slice: x: 2, y: 2, z: 4, core: 2. Of those that a mesh axis runs over, the one named last changes fastest.
Arguments:
- tokens: bfloat16 [16384, 1024], P('dp'), may hold values from -6 to 6
- segment_ids: int32 [16384], P('dp'), may hold values from 0 to 127, as said below
- attn_gain: bfloat16 [1024], P('dp'), may hold values from 0.5 to 1.5
- w_qkv: bfloat16 [1024, 3, 1024], P('dp', None, 'mp'), may hold values from -6 to 6
- w_out: bfloat16 [1024, 1024], P('mp', 'dp'), may hold values from -0.5 to 0.5
- mlp_gain: bfloat16 [1024], P('dp'), may hold values from 0.5 to 1.5
- w_in: bfloat16 [1024, 2, 2624], P('dp', None, 'mp'), may hold values from -0.1875 to 0.1875
- w_ff_out: bfloat16 [2624, 1024], P('mp', 'dp'), may hold values from -0.125 to 0.125
- cotangent: bfloat16 [16384, 1024], P('dp'), may hold values from -6 to 6
Outputs:
- output: bfloat16 [16384, 1024], P('dp')
- input_grad: float32 [16384, 1024], P('dp')
- attn_gain_grad: float32 [1024], P('dp')
- qkv_grad: float32 [1024, 3, 1024], P('dp', None, 'mp')
- out_grad: float32 [1024, 1024], P('mp', 'dp')
- mlp_gain_grad: float32 [1024], P('dp')
- in_grad: float32 [1024, 2, 2624], P('dp', None, 'mp')
- ff_out_grad: float32 [2624, 1024], P('mp', 'dp')
The draws below stay inside these ranges and needn't reach their ends.
Inputs may be any that keep to these rules, and one draw needn't show every extreme that they name: `segment_ids`: within each aligned block of 1024 tokens (those of one index of dp) the segment numbers start at 0 and never fall; equal numbers form one sequence; a new sequence begins only at a position inside the block that is a multiple of 8, and some block is cut at every such position.
All inputs are finite; a program needn't handle non-finite values.
Results may differ from the reference program's by a relative error of at most 0.025.
Values may be sent and summed in bfloat16 or wider, within the bound.
No kernel may reach another device: no remote copies, remote signals or barrier semaphores. Data moves between devices by JAX's collectives and lax.ppermute only.
A program may use at most 256 MiB of HBM per device.

```python
import jax
import jax.numpy as jnp
from jax import lax

D = 1024
HEADS = 16
HD = 64
FF = 2624
TOK_DEV = 1024
TOKENS = 16384
N_DP = 16
N_MP = 2


def draw_segment_ids(key, part):
    first_key, second_key, third_key = jax.random.split(jax.random.fold_in(key, 11), 3)
    row_count = TOKENS // TOK_DEV
    level = jax.random.randint(first_key, (row_count,), 0, 4)
    limits = jnp.array([0, 32, 64, 256], jnp.int32)[level]
    forced_row = jax.random.randint(third_key, (), 0, row_count)
    rows_index = jnp.arange(row_count, dtype=jnp.int32)
    limits = jnp.where(rows_index == forced_row, 256, limits)
    cuts = jax.random.randint(second_key, (row_count, TOK_DEV), 0, 256) < limits[:, None]
    position = jnp.arange(TOK_DEV, dtype=jnp.int32)[None, :]
    allowed_cut = jnp.logical_and(position > 0, position % 8 == 0)
    cuts = jnp.logical_and(cuts, allowed_cut)
    segment_ids = jnp.cumsum(cuts.astype(jnp.int32), axis=1)
    return segment_ids.reshape(TOKENS).astype(jnp.int32)


def draw_w_qkv(key, part):
    first_key = jax.random.fold_in(jax.random.fold_in(key, 23), 0)
    base = jax.random.normal(first_key, (D, 3, D), jnp.float32) * D ** (-0.5)
    return jnp.clip(base, -6.0, 6.0).astype(jnp.bfloat16)


def with_spikes(values, rng, source, target, blocks, factor):
    def block_of(dim):
        return (jnp.arange(values.shape[dim]) // (values.shape[dim] // blocks)).reshape((-1,) + (1,) * (values.ndim - 1 - dim))

    first = jax.random.permutation(rng, blocks)[block_of(target)]
    second = (block_of(target) + blocks // 2) % blocks
    return jnp.where((block_of(source) == first) | (block_of(source) == second), factor * values, values)


def block_scale(rng, dims, shards, low, top_value):
    level, own = 1.0, jax.random.fold_in(rng, 6)
    for dim, blocks in shards:
        steps = jnp.exp(jax.random.uniform(jax.random.fold_in(own, dim), (blocks,), jnp.float32, low / len(shards), top_value / len(shards)))
        level = level * jnp.repeat(steps, dims[dim] // blocks).reshape([-1 if axis == dim else 1 for axis in range(len(dims))])
    return level


def normal_values(key, shape, deviation, reach, cuts=(), kind=jnp.bfloat16):
    entries = jax.random.normal(key, shape, jnp.float32) * deviation
    if len(cuts) > 0:
        entries = block_scale(key, shape, cuts, -0.22, 0.18) * entries
    return jnp.clip(entries, min=-reach, max=reach).astype(kind)


def bell_draw_with(own_key, shape, deviation, limit, shards, heavy, held_as=jnp.bfloat16):
    drawn = deviation * jax.random.normal(own_key, shape, jnp.float32)
    if shards:
        drawn = drawn * block_scale(own_key, shape, shards, -0.22, 0.18)
    return jnp.clip(with_spikes(drawn, jax.random.fold_in(own_key, 3), *heavy), -limit, limit).astype(held_as)


def setup_inputs(seed: int = 0) -> dict:
    arg_keys = jax.random.split(jax.random.key(seed), 10)
    tokens = bell_draw_with(arg_keys[0], (TOKENS, D), 1.0, 6.0, ((0, 16),), (0, 1, 16, 2.0))
    segment_ids = draw_segment_ids(jax.random.fold_in(arg_keys[9], 71), 0)
    attn_gain = jnp.clip(1.0 + 0.1 * jax.random.normal(arg_keys[2], (D,), jnp.float32), 0.5, 1.5).astype(jnp.bfloat16)
    w_qkv = draw_w_qkv(jax.random.fold_in(arg_keys[9], 71), 0)
    w_out = normal_values(arg_keys[4], (D, D), (D // 8) ** -0.5, 0.5, ((0, 2), (1, 16)))
    mlp_gain = jnp.clip(1.0 + 0.1 * jax.random.normal(arg_keys[5], (D,), jnp.float32), 0.5, 1.5).astype(jnp.bfloat16)
    w_in = normal_values(arg_keys[6], (D, 2, FF), D ** -0.5, 0.1875, ((0, 16), (2, 2)))
    w_ff_out = normal_values(arg_keys[7], (FF, D), FF ** -0.5, 0.125, ((0, 2), (1, 16)))
    cotangent = bell_draw_with(arg_keys[8], (TOKENS, D), 1.0, 6.0, ((0, 16),), (0, 1, 16, 2.0))
    return {"tokens": tokens, "segment_ids": segment_ids, "attn_gain": attn_gain, "w_qkv": w_qkv, "w_out": w_out, "mlp_gain": mlp_gain, "w_in": w_in, "w_ff_out": w_ff_out, "cotangent": cotangent}


EPSILON = 1e-05
ROPE_BASE = 160000.0
NEGATIVE = -1e+30

def normalize(values):
    center = values - lax.optimization_barrier(jnp.mean(values, axis=-1, keepdims=True))
    inverse = lax.rsqrt(lax.optimization_barrier(jnp.mean(center * center, axis=-1, keepdims=True)) + EPSILON)
    return (center * inverse, inverse)

def norm_back(gradient, normed, inverse, gain_vec):
    scaled = gradient * gain_vec
    return inverse * (scaled - lax.optimization_barrier(jnp.mean(scaled, axis=-1, keepdims=True)) - normed * lax.optimization_barrier(jnp.mean(scaled * normed, axis=-1, keepdims=True)))

def positions(segment_ids):
    index_row = jnp.arange(segment_ids.shape[0], dtype=jnp.int32)
    change = jnp.concatenate([jnp.ones((1,), bool), segment_ids[1:] != segment_ids[:-1]])
    marker = jnp.where(change, index_row, jnp.zeros_like(index_row)).astype(jnp.int32)
    starts = lax.cummax(marker, axis=0)
    return (index_row - starts).astype(jnp.float32)

def rope_tables(places, head_size):
    half_size = head_size // 2
    inverse = ROPE_BASE ** (-2.0 * jnp.arange(half_size, dtype=jnp.float32) / head_size)
    angles = places[:, None] * inverse[None, :]
    return (jnp.cos(angles)[:, None, :], jnp.sin(angles)[:, None, :])

def rotate(values, cosine, sine_table):
    half_size = values.shape[-1] // 2
    front_half, back_half = (values[..., :half_size], values[..., half_size:])
    return jnp.concatenate([front_half * cosine - back_half * sine_table, back_half * cosine + front_half * sine_table], axis=-1)

def unrotate(gradient, cosine, sine_table):
    half_size = gradient.shape[-1] // 2
    front_half, back_half = (gradient[..., :half_size], gradient[..., half_size:])
    return jnp.concatenate([front_half * cosine + back_half * sine_table, back_half * cosine - front_half * sine_table], axis=-1)

def gelu_grad(values):
    return 0.5 * (1.0 + lax.erf(values * 0.7071067811865476)) + values * jnp.exp(-0.5 * values * values) * 0.3989422804014327

def masked_scores(queries, keys_rot, allowed, score_scale):
    scores = jnp.einsum('qhd,khd->hqk', queries.astype(jnp.float32), keys_rot.astype(jnp.float32)) * score_scale
    return jnp.where(allowed[None], scores, NEGATIVE)

def one_block(tokens, segment_ids, cotangent, attn_gain, w_qkv, w_out, mlp_gain, w_in, w_ff_out):
    rows_here = tokens.shape[0]
    groups = N_MP
    score_scale = HD ** (-0.5)
    gain_one = attn_gain.astype(jnp.float32)
    gain_two = mlp_gain.astype(jnp.float32)
    resid = tokens.astype(jnp.float32)
    normed_one, inverse_one = normalize(resid)
    hidden_one = (normed_one * gain_one).astype(jnp.bfloat16)
    projected = jnp.einsum('td,dcf->tcf', hidden_one.astype(jnp.float32), w_qkv.astype(jnp.float32))
    cosine, sine_table = rope_tables(positions(segment_ids), HD)
    allowed = segment_ids[:, None] == segment_ids[None, :]
    queries = rotate(projected[:, 0].reshape(rows_here, HEADS, HD), cosine, sine_table).astype(jnp.bfloat16)
    keys_rot = rotate(projected[:, 1].reshape(rows_here, HEADS, HD), cosine, sine_table).astype(jnp.bfloat16)
    values = projected[:, 2].reshape(rows_here, HEADS, HD).astype(jnp.bfloat16)
    scores = masked_scores(queries, keys_rot, allowed, score_scale)
    row_peak = lax.optimization_barrier(jnp.max(scores, axis=-1, keepdims=True))
    log_total = row_peak + jnp.log(lax.optimization_barrier(jnp.sum(jnp.exp(scores - row_peak), axis=-1, keepdims=True)))
    attn_probs = jnp.exp(scores - log_total)
    rounded_probs = attn_probs.astype(jnp.bfloat16)
    context = jnp.einsum('hqk,khd->qhd', rounded_probs.astype(jnp.float32), values.astype(jnp.float32)).astype(jnp.bfloat16)
    context_flat = context.reshape(rows_here, D)
    attn_parts = jnp.einsum('tgf,gfd->gtd', context_flat.reshape(rows_here, groups, D // groups).astype(jnp.float32), w_out.reshape(groups, D // groups, D).astype(jnp.float32))
    attn_out = lax.optimization_barrier(jnp.sum(attn_parts.astype(jnp.bfloat16).astype(jnp.float32), axis=0))
    middle = resid + attn_out
    normed_two, inverse_two = normalize(middle)
    hidden_two = (normed_two * gain_two).astype(jnp.bfloat16)
    gate_up = jnp.einsum('td,dcf->tcf', hidden_two.astype(jnp.float32), w_in.astype(jnp.float32))
    gate_pre, upward = (gate_up[:, 0], gate_up[:, 1])
    active = jax.nn.gelu(gate_pre, approximate=False)
    mixed_act = (active * upward).astype(jnp.bfloat16)
    ffn_parts = jnp.einsum('tgf,gfd->gtd', mixed_act.reshape(rows_here, groups, FF // groups).astype(jnp.float32), w_ff_out.reshape(groups, FF // groups, D).astype(jnp.float32))
    ffn_out = lax.optimization_barrier(jnp.sum(ffn_parts.astype(jnp.bfloat16).astype(jnp.float32), axis=0))
    output = (middle + ffn_out).astype(jnp.bfloat16)
    upstream = cotangent.astype(jnp.float32)
    ffo_grad = jnp.dot(mixed_act.T, cotangent, preferred_element_type=jnp.float32)
    mixed_grad = jnp.dot(cotangent, w_ff_out.T, preferred_element_type=jnp.float32)
    gate_up_grad = jnp.stack([mixed_grad * upward * gelu_grad(gate_pre), mixed_grad * active], axis=1).astype(jnp.bfloat16)
    in_grad = jnp.einsum('td,tcf->dcf', hidden_two.astype(jnp.float32), gate_up_grad.astype(jnp.float32))
    two_parts = jnp.einsum('tcgf,dcgf->gtd', gate_up_grad.reshape(rows_here, 2, groups, FF // groups).astype(jnp.float32), w_in.reshape(D, 2, groups, FF // groups).astype(jnp.float32))
    hidden_two_grad = lax.optimization_barrier(jnp.sum(two_parts.astype(jnp.bfloat16).astype(jnp.float32), axis=0))
    gain_two_grad = lax.optimization_barrier(jnp.sum(hidden_two_grad * normed_two, axis=0))
    middle_grad = upstream + norm_back(hidden_two_grad, normed_two, inverse_two, gain_two)
    attn_grad_in = middle_grad.astype(jnp.bfloat16)
    out_grad = jnp.dot(context_flat.T, attn_grad_in, preferred_element_type=jnp.float32)
    context_grad = jnp.dot(attn_grad_in, w_out.T, preferred_element_type=jnp.float32).astype(jnp.bfloat16).reshape(rows_here, HEADS, HD)
    value_grad = jnp.einsum('hqk,qhd->khd', rounded_probs.astype(jnp.float32), context_grad.astype(jnp.float32))
    prob_grad = jnp.einsum('qhd,khd->hqk', context_grad.astype(jnp.float32), values.astype(jnp.float32))
    delta_row = lax.optimization_barrier(jnp.sum(attn_probs * prob_grad, axis=-1, keepdims=True))
    score_grad = (attn_probs * (prob_grad - delta_row)).astype(jnp.bfloat16).astype(jnp.float32)
    query_grad = jnp.einsum('hqk,khd->qhd', score_grad, keys_rot.astype(jnp.float32)) * score_scale
    key_grad = jnp.einsum('hqk,qhd->khd', score_grad, queries.astype(jnp.float32)) * score_scale
    projected_grad = jnp.stack([unrotate(query_grad, cosine, sine_table).reshape(rows_here, D), unrotate(key_grad, cosine, sine_table).reshape(rows_here, D), value_grad.reshape(rows_here, D)], axis=1).astype(jnp.bfloat16)
    qkv_grad = jnp.einsum('td,tcf->dcf', hidden_one.astype(jnp.float32), projected_grad.astype(jnp.float32))
    one_parts = jnp.einsum('tcgf,dcgf->gtd', projected_grad.reshape(rows_here, 3, groups, D // groups).astype(jnp.float32), w_qkv.reshape(D, 3, groups, D // groups).astype(jnp.float32))
    hidden_one_grad = lax.optimization_barrier(jnp.sum(one_parts.astype(jnp.bfloat16).astype(jnp.float32), axis=0))
    gain_one_grad = lax.optimization_barrier(jnp.sum(hidden_one_grad * normed_one, axis=0))
    input_grad = middle_grad + norm_back(hidden_one_grad, normed_one, inverse_one, gain_one)
    return (output, input_grad, (gain_one_grad, qkv_grad, out_grad, gain_two_grad, in_grad, ffo_grad))

def reference(tokens, segment_ids, attn_gain, w_qkv, w_out, mlp_gain, w_in, w_ff_out, cotangent):
    blocks = (tokens.reshape(N_DP, TOK_DEV, D), segment_ids.reshape(N_DP, TOK_DEV), cotangent.reshape(N_DP, TOK_DEV, D))
    initial = (jnp.zeros((D,), jnp.float32), jnp.zeros((D, 3, D), jnp.float32), jnp.zeros((D, D), jnp.float32), jnp.zeros((D,), jnp.float32), jnp.zeros((D, 2, FF), jnp.float32), jnp.zeros((FF, D), jnp.float32))

    def advance(carry, pieces):
        output, input_grad, gradients = one_block(pieces[0], pieces[1], pieces[2], attn_gain, w_qkv, w_out, mlp_gain, w_in, w_ff_out)
        return (tuple((total + extra for total, extra in zip(carry, gradients))), (output, input_grad))
    totals, stacked = lax.scan(advance, initial, blocks)
    return (stacked[0].reshape(TOKENS, D), stacked[1].reshape(TOKENS, D), totals[0], totals[1], totals[2], totals[3], totals[4], totals[5])
```

```python
import functools

import jax
import jax.numpy as jnp
from jax import lax
from jax.experimental import pallas as pl
from jax.experimental.pallas import tpu as pltpu
from jax.sharding import PartitionSpec as P

HD = 64
LANES = 128
EPSILON = 1e-05
ROPE_BASE = 160000.0
NEGATIVE = -1e30
VMEM_BYTES = 60 * 1024 * 1024


def contract(left, right, left_axis, right_axis, **kwargs):
    return lax.dot_general(
        left, right, (((left_axis,), (right_axis,)), ((), ())), preferred_element_type=jnp.float32, **kwargs
    )


def lane_of(rows):
    return lax.broadcasted_iota(jnp.int32, (rows, LANES), 1)


def partner(values):
    front = lane_of(values.shape[0]) % HD < HD // 2
    return jnp.where(
        front, pltpu.roll(values, LANES - HD // 2, 1), pltpu.roll(values, HD // 2, 1)
    )


def rotate(values, cosine, signed_sine):
    return values * cosine + partner(values) * signed_sine


def unrotate(gradient, cosine, signed_sine):
    return gradient * cosine - partner(gradient) * signed_sine


def attend_kernel(
    heads, query_ref, key_ref, value_ref, cos_tile, sin_tile, cos_ref, sin_ref, seg_col, seg_row, out_w,
    *refs,
):
    context_ref, total_ref, partial_ref, keys, values = refs[-5:]
    score_scale = HD ** (-0.5)

    @pl.when(pl.program_id(0) == 0)
    def _():
        for pair in range(heads // 2):
            cols = slice(pair * LANES, (pair + 1) * LANES)
            keys[:, cols] = rotate(key_ref[:, cols], cos_ref[...], sin_ref[...]).astype(jnp.bfloat16)
        values[...] = value_ref[...].astype(jnp.bfloat16)

    rows = query_ref.shape[0]
    lane = lane_of(rows)
    allowed = seg_col[...] == seg_row[...]
    totals = jnp.zeros((rows, LANES), jnp.float32)
    for pair in range(heads // 2):
        cols = slice(pair * LANES, (pair + 1) * LANES)
        query = rotate(query_ref[:, cols], cos_tile[...], sin_tile[...]) * score_scale
        context = jnp.zeros((rows, LANES), jnp.float32)
        for half in range(2):
            own = lane // HD == half
            scores = contract(jnp.where(own, query, 0.0).astype(jnp.bfloat16), keys[:, cols], 1, 1)
            scores = jnp.where(allowed, scores, NEGATIVE)
            peak = jnp.max(scores, axis=-1, keepdims=True)
            weights = jnp.exp(scores - peak)
            total = jnp.sum(weights, axis=-1, keepdims=True)
            mixed = contract(weights.astype(jnp.bfloat16), values[:, cols], 1, 0)
            context = jnp.where(own, mixed / total, context)
            totals = jnp.where(lane == 2 * pair + half, peak + jnp.log(total), totals)
        context_ref[:, cols] = context.astype(jnp.bfloat16)
    total_ref[...] = totals.T[:heads]
    partial_ref[...] = contract(context_ref[...], out_w[...], 1, 1).astype(jnp.bfloat16)


def attend(projected, tables, seg_col, seg_row, out_w, start, rows, tile, earlier=()):
    count, width = projected.shape[0], projected.shape[1] // 3
    heads, model = width // HD, out_w.shape[0]
    first = start // tile
    fixed = dict(pipeline_mode=pl.Buffered(1))
    return pl.pallas_call(
        functools.partial(attend_kernel, heads),
        grid=(rows // tile,),
        in_specs=[
            pl.BlockSpec((tile, width), lambda i: (first + i, 0)),
            pl.BlockSpec((count, width), lambda i: (0, 1), **fixed),
            pl.BlockSpec((count, width), lambda i: (0, 2), **fixed),
            pl.BlockSpec((tile, LANES), lambda i: (first + i, 0)),
            pl.BlockSpec((tile, LANES), lambda i: (first + i, 0)),
            pl.BlockSpec((count, LANES), lambda i: (0, 0), **fixed),
            pl.BlockSpec((count, LANES), lambda i: (0, 0), **fixed),
            pl.BlockSpec((tile, 1), lambda i: (first + i, 0)),
            pl.BlockSpec((1, count), lambda i: (0, 0), **fixed),
            pl.BlockSpec((model, width), lambda i: (0, 0), **fixed),
        ]
        + [pl.BlockSpec(memory_space=pl.ANY)] * len(earlier),
        out_specs=[
            pl.BlockSpec((tile, width), lambda i: (first + i, 0)),
            pl.BlockSpec((heads, tile), lambda i: (0, first + i)),
            pl.BlockSpec((tile, model), lambda i: (i, 0)),
        ],
        out_shape=[
            jax.ShapeDtypeStruct((count, width), jnp.bfloat16),
            jax.ShapeDtypeStruct((heads, count), jnp.float32),
            jax.ShapeDtypeStruct((rows, model), jnp.bfloat16),
        ],
        input_output_aliases={10 + at: at for at in range(len(earlier))},
        scratch_shapes=[pltpu.VMEM((count, width), jnp.bfloat16), pltpu.VMEM((count, width), jnp.bfloat16)],
        compiler_params=pltpu.CompilerParams(vmem_limit_bytes=VMEM_BYTES),
        cost_estimate=pl.CostEstimate(
            flops=4 * rows * count * width * 2 + 2 * rows * width * model,
            bytes_accessed=4 * count * width * 3 + 2 * model * width + 2 * rows * (model + width),
            transcendentals=rows * count * heads,
        ),
        name="attend",
    )(projected, projected, projected, *tables, *tables, seg_col, seg_row, out_w, *earlier)


def attend_back_kernel(
    query_ref, key_ref, value_ref, cos_tile, sin_tile, cos_ref, sin_ref, seg_col, seg_row,
    upstream_ref, context_ref, total_ref, grad_ref, keys, values, key_grad, value_grad,
):
    score_scale = HD ** (-0.5)
    pair, step = pl.program_id(0), pl.program_id(1)

    @pl.when(step == 0)
    def _():
        keys[...] = rotate(key_ref[...], cos_ref[...], sin_ref[...]).astype(jnp.bfloat16)
        values[...] = value_ref[...].astype(jnp.bfloat16)
        key_grad[...] = jnp.zeros_like(key_grad)
        value_grad[...] = jnp.zeros_like(value_grad)

    rows = query_ref.shape[0]
    lane = lane_of(rows)
    allowed = seg_col[...] == seg_row[...]
    query = rotate(query_ref[...], cos_tile[...], sin_tile[...]) * score_scale
    upstream = upstream_ref[...].astype(jnp.float32)
    product = upstream * context_ref[...].astype(jnp.float32)
    query_grad = jnp.zeros((rows, LANES), jnp.float32)
    for half in range(2):
        own = lane // HD == half
        own_query = jnp.where(own, query, 0.0).astype(jnp.bfloat16)
        own_upstream = jnp.where(own, upstream, 0.0).astype(jnp.bfloat16)
        picks = (lane_of(8) // HD == half).astype(jnp.float32)
        delta = contract(picks, product, 1, 1, precision=lax.Precision.HIGHEST)[0:1]
        total = total_ref[pl.ds(2 * pair + half, 1), :]
        scores = contract(keys[...], own_query, 1, 1)
        probs = jnp.where(allowed, jnp.exp(scores - total), 0.0)
        prob_grad = contract(values[...], own_upstream, 1, 1)
        score_grad = (probs * (prob_grad - delta)).astype(jnp.bfloat16)
        value_grad[...] += contract(probs.astype(jnp.bfloat16), own_upstream, 1, 0)
        key_grad[...] += contract(score_grad, own_query, 1, 0)
        spread = contract(score_grad, keys[...], 0, 0)
        query_grad = jnp.where(own, spread, query_grad)
    at = pl.ds(pl.multiple_of(step * rows, rows), rows)
    grad_ref[0, at, :] = unrotate(query_grad * score_scale, cos_tile[...], sin_tile[...]).astype(jnp.bfloat16)

    @pl.when(step == pl.num_programs(1) - 1)
    def _():
        grad_ref[1] = unrotate(key_grad[...], cos_ref[...], sin_ref[...]).astype(jnp.bfloat16)
        grad_ref[2] = value_grad[...].astype(jnp.bfloat16)


def attend_back(projected, tables, seg_col, seg_row, upstream, context, totals, tile):
    count, width = projected.shape[0], projected.shape[1] // 3
    heads, pairs = width // HD, width // LANES
    fixed = dict(pipeline_mode=pl.Buffered(1))
    return pl.pallas_call(
        attend_back_kernel,
        grid=(pairs, count // tile),
        in_specs=[
            pl.BlockSpec((tile, LANES), lambda p, i: (i, p)),
            pl.BlockSpec((count, LANES), lambda p, i: (0, pairs + p)),
            pl.BlockSpec((count, LANES), lambda p, i: (0, 2 * pairs + p)),
            pl.BlockSpec((tile, LANES), lambda p, i: (i, 0)),
            pl.BlockSpec((tile, LANES), lambda p, i: (i, 0)),
            pl.BlockSpec((count, LANES), lambda p, i: (0, 0), **fixed),
            pl.BlockSpec((count, LANES), lambda p, i: (0, 0), **fixed),
            pl.BlockSpec((count, 1), lambda p, i: (0, 0), **fixed),
            pl.BlockSpec((1, tile), lambda p, i: (0, i)),
            pl.BlockSpec((tile, LANES), lambda p, i: (i, p)),
            pl.BlockSpec((tile, LANES), lambda p, i: (i, p)),
            pl.BlockSpec((heads, tile), lambda p, i: (0, i)),
        ],
        out_specs=pl.BlockSpec((3, count, LANES), lambda p, i: (0, 0, p)),
        out_shape=jax.ShapeDtypeStruct((3, count, width), jnp.bfloat16),
        scratch_shapes=[
            pltpu.VMEM((count, LANES), jnp.bfloat16),
            pltpu.VMEM((count, LANES), jnp.bfloat16),
            pltpu.VMEM((count, LANES), jnp.float32),
            pltpu.VMEM((count, LANES), jnp.float32),
        ],
        compiler_params=pltpu.CompilerParams(vmem_limit_bytes=VMEM_BYTES),
        cost_estimate=pl.CostEstimate(
            flops=10 * count * count * width * 2,
            bytes_accessed=4 * count * width * 3 + 2 * count * width * 5,
            transcendentals=count * count * heads,
        ),
        name="attend_back",
    )(projected, projected, projected, *tables, *tables, seg_col, seg_row, upstream, context, totals)


def feed_kernel(
    tokens_ref, own_ref, other_ref, cot_ref, gain_ref, gate_w, up_w, down_w,
    *refs,
):
    hidden_ref, acts_ref, out_ref, grad_ref, gain_grad_ref = refs[-5:]
    middle = tokens_ref[...].astype(jnp.float32) + (
        own_ref[...].astype(jnp.float32) + other_ref[...].astype(jnp.float32)
    )
    center = middle - jnp.mean(middle, axis=-1, keepdims=True)
    normed = center * lax.rsqrt(jnp.mean(center * center, axis=-1, keepdims=True) + EPSILON)
    hidden = (normed * gain_ref[...]).astype(jnp.bfloat16)
    hidden_ref[...] = hidden
    gate = contract(hidden, gate_w[...], 1, 0)
    upward = contract(hidden, up_w[...], 1, 0)
    mixed_grad = contract(cot_ref[...], down_w[...], 1, 0)
    share = 0.5 * (1.0 + lax.erf(gate * 0.7071067811865476))
    active = gate * share
    slope = share + gate * jnp.exp(-0.5 * gate * gate) * 0.3989422804014327
    size = gate.shape[1]
    gate_grad = (mixed_grad * upward * slope).astype(jnp.bfloat16)
    up_grad = (mixed_grad * active).astype(jnp.bfloat16)
    mixed = (active * upward).astype(jnp.bfloat16)
    acts_ref[:, :size] = gate_grad
    acts_ref[:, size : 2 * size] = up_grad
    acts_ref[:, 2 * size :] = mixed
    out_ref[...] = contract(mixed, down_w[...], 1, 1).astype(jnp.bfloat16)
    partial = contract(gate_grad, gate_w[...], 1, 1) + contract(up_grad, up_w[...], 1, 1)
    grad_ref[...] = partial.astype(jnp.bfloat16)

    @pl.when(pl.program_id(0) == 0)
    def _():
        gain_grad_ref[...] = jnp.zeros_like(gain_grad_ref)

    gain_grad_ref[...] += jnp.sum(partial * normed, axis=0, keepdims=True)


def feed(tokens, own, other, cotangent, gain, ffn_full, start, tile, earlier=()):
    rows, model = own.shape
    size = ffn_full.shape[1] // 3
    first = start // tile
    fixed = dict(pipeline_mode=pl.Buffered(1))
    row_block = pl.BlockSpec((tile, model), lambda i: (i, 0))
    late_block = pl.BlockSpec((tile, model), lambda i: (first + i, 0))
    return pl.pallas_call(
        feed_kernel,
        grid=(rows // tile,),
        in_specs=[
            late_block, row_block, row_block, late_block,
            pl.BlockSpec((1, model), lambda i: (0, 0), **fixed),
            pl.BlockSpec((model, size), lambda i: (0, 0), **fixed),
            pl.BlockSpec((model, size), lambda i: (0, 1), **fixed),
            pl.BlockSpec((model, size), lambda i: (0, 2), **fixed),
        ]
        + [pl.BlockSpec(memory_space=pl.ANY)] * len(earlier),
        out_specs=[
            late_block,
            pl.BlockSpec((tile, 3 * size), lambda i: (first + i, 0)),
            row_block, row_block,
            pl.BlockSpec((1, model), lambda i: (0, 0)),
        ],
        out_shape=[
            jax.ShapeDtypeStruct(tokens.shape, jnp.bfloat16),
            jax.ShapeDtypeStruct((tokens.shape[0], 3 * size), jnp.bfloat16),
            jax.ShapeDtypeStruct((rows, model), jnp.bfloat16),
            jax.ShapeDtypeStruct((rows, model), jnp.bfloat16),
            jax.ShapeDtypeStruct((1, model), jnp.float32),
        ],
        input_output_aliases={8 + at: at for at in range(len(earlier))},
        compiler_params=pltpu.CompilerParams(vmem_limit_bytes=VMEM_BYTES),
        cost_estimate=pl.CostEstimate(
            flops=12 * rows * model * size,
            bytes_accessed=2 * (3 * model * size + 7 * rows * model + 3 * rows * size),
            transcendentals=2 * rows * size,
        ),
        name="feed",
    )(tokens, own, other, cotangent, gain, ffn_full, ffn_full, ffn_full, *earlier)


def assemble_kernel(count, places_ref, *refs):
    rows = refs[0].shape[0]
    for index in range(count):
        at = pl.multiple_of(places_ref[index] * rows, rows)
        begin = 0
        for out_ref in refs[count:]:
            end = begin + out_ref.shape[1]
            out_ref[pl.ds(at, rows), :] = refs[index][:, begin:end]
            begin = end


def assemble(pieces, places, widths):
    count = len(pieces)
    rows, width = pieces[0].shape
    whole = pl.BlockSpec(memory_space=pltpu.VMEM)
    return pl.pallas_call(
        functools.partial(assemble_kernel, count),
        in_specs=[pl.BlockSpec(memory_space=pltpu.SMEM)] + [whole] * count,
        out_specs=[whole] * len(widths),
        out_shape=[jax.ShapeDtypeStruct((count * rows, each), pieces[0].dtype) for each in widths],
        compiler_params=pltpu.CompilerParams(vmem_limit_bytes=VMEM_BYTES),
        cost_estimate=pl.CostEstimate(flops=0, bytes_accessed=4 * count * rows * width, transcendentals=0),
        name="assemble",
    )(places, *pieces)


def middle_back_kernel(
    tokens_ref, own_ref, other_ref, own_grad_ref, other_grad_ref, cot_ref, gain_ref, out_w, grad_ref, context_grad_ref
):
    middle = tokens_ref[...].astype(jnp.float32) + (
        own_ref[...].astype(jnp.float32) + other_ref[...].astype(jnp.float32)
    )
    center = middle - jnp.mean(middle, axis=-1, keepdims=True)
    inverse = lax.rsqrt(jnp.mean(center * center, axis=-1, keepdims=True) + EPSILON)
    normed = center * inverse
    scaled = (own_grad_ref[...].astype(jnp.float32) + other_grad_ref[...].astype(jnp.float32)) * gain_ref[...]
    back = inverse * (
        scaled
        - jnp.mean(scaled, axis=-1, keepdims=True)
        - normed * jnp.mean(scaled * normed, axis=-1, keepdims=True)
    )
    gradient = (cot_ref[...].astype(jnp.float32) + back).astype(jnp.bfloat16)
    grad_ref[...] = gradient
    context_grad_ref[...] = contract(gradient, out_w[...], 1, 0).astype(jnp.bfloat16)


def middle_back(tokens, own, other, own_grad, other_grad, cotangent, gain, out_w, start, tile, earlier=()):
    rows, model = own.shape
    width, first = out_w.shape[1], start // tile
    fixed = dict(pipeline_mode=pl.Buffered(1))
    row_block = pl.BlockSpec((tile, model), lambda i: (i, 0))
    late_block = pl.BlockSpec((tile, model), lambda i: (first + i, 0))

    def body(*refs):
        middle_back_kernel(*refs[:8], *refs[-2:])

    return pl.pallas_call(
        body,
        grid=(rows // tile,),
        in_specs=[
            late_block, row_block, row_block, row_block, row_block, late_block,
            pl.BlockSpec((1, model), lambda i: (0, 0), **fixed),
            pl.BlockSpec((model, width), lambda i: (0, 0), **fixed),
        ]
        + [pl.BlockSpec(memory_space=pl.ANY)] * len(earlier),
        out_specs=[late_block, pl.BlockSpec((tile, width), lambda i: (first + i, 0))],
        out_shape=[
            jax.ShapeDtypeStruct(tokens.shape, jnp.bfloat16),
            jax.ShapeDtypeStruct((tokens.shape[0], width), jnp.bfloat16),
        ],
        input_output_aliases={8 + at: at for at in range(len(earlier))},
        compiler_params=pltpu.CompilerParams(vmem_limit_bytes=VMEM_BYTES),
        cost_estimate=pl.CostEstimate(
            flops=2 * rows * model * width, bytes_accessed=2 * (7 * rows * model + model * width), transcendentals=0
        ),
        name="middle_back",
    )(tokens, own, other, own_grad, other_grad, cotangent, gain, out_w, *earlier)


def last_kernel(tokens_ref, own_grad_ref, other_grad_ref, above_ref, gain_ref, grad_ref):
    values = tokens_ref[...].astype(jnp.float32)
    center = values - jnp.mean(values, axis=-1, keepdims=True)
    inverse = lax.rsqrt(jnp.mean(center * center, axis=-1, keepdims=True) + EPSILON)
    normed = center * inverse
    scaled = (own_grad_ref[...].astype(jnp.float32) + other_grad_ref[...].astype(jnp.float32)) * gain_ref[...]
    back = inverse * (
        scaled
        - jnp.mean(scaled, axis=-1, keepdims=True)
        - normed * jnp.mean(scaled * normed, axis=-1, keepdims=True)
    )
    grad_ref[...] = above_ref[...].astype(jnp.float32) + back


def last(tokens, own_grad, other_grad, above, gain, start, tile, earlier=()):
    rows, model = own_grad.shape
    first = start // tile
    row_block = pl.BlockSpec((tile, model), lambda i: (i, 0))
    late_block = pl.BlockSpec((tile, model), lambda i: (first + i, 0))

    def body(*refs):
        last_kernel(*refs[:5], refs[-1])

    return pl.pallas_call(
        body,
        grid=(rows // tile,),
        in_specs=[late_block, row_block, row_block, late_block, pl.BlockSpec((1, model), lambda i: (0, 0))]
        + [pl.BlockSpec(memory_space=pl.ANY)] * len(earlier),
        out_specs=late_block,
        out_shape=jax.ShapeDtypeStruct(tokens.shape, jnp.float32),
        input_output_aliases={5 + at: at for at in range(len(earlier))},
        compiler_params=pltpu.CompilerParams(vmem_limit_bytes=VMEM_BYTES),
        cost_estimate=pl.CostEstimate(flops=20 * rows * model, bytes_accessed=12 * rows * model, transcendentals=0),
        name="last",
    )(tokens, own_grad, other_grad, above, gain, *earlier)


def feed_weights_kernel(hidden_ref, cot_ref, acts_ref, out_ref):
    @pl.when(pl.program_id(0) < 2)
    def _():
        out_ref[...] = contract(hidden_ref[...], acts_ref[...], 0, 0).astype(jnp.bfloat16)

    @pl.when(pl.program_id(0) == 2)
    def _():
        out_ref[...] = contract(cot_ref[...], acts_ref[...], 0, 0).astype(jnp.bfloat16)


def feed_weights(hidden, cotangent, acts, tile):
    count, model = hidden.shape
    size = acts.shape[1] // 3
    return pl.pallas_call(
        feed_weights_kernel,
        grid=(3, model // tile),
        in_specs=[
            pl.BlockSpec((count, tile), lambda j, i: (0, i)),
            pl.BlockSpec((count, tile), lambda j, i: (0, i)),
            pl.BlockSpec((count, size), lambda j, i: (0, j)),
        ],
        out_specs=pl.BlockSpec((tile, size), lambda j, i: (i, j)),
        out_shape=jax.ShapeDtypeStruct((model, 3 * size), jnp.bfloat16),
        compiler_params=pltpu.CompilerParams(vmem_limit_bytes=VMEM_BYTES),
        cost_estimate=pl.CostEstimate(
            flops=6 * count * model * size, bytes_accessed=6 * count * size + 4 * count * model + 6 * model * size,
            transcendentals=0,
        ),
        name="feed_weights",
    )(hidden, cotangent, acts)


def positions(segment_ids):
    index_row = jnp.arange(segment_ids.shape[0], dtype=jnp.int32)
    change = jnp.concatenate([jnp.ones((1,), bool), segment_ids[1:] != segment_ids[:-1]])
    marker = jnp.where(change, index_row, jnp.zeros_like(index_row))
    starts = lax.cummax(marker, axis=0)
    return (index_row - starts).astype(jnp.float32)


def rope_tables(places):
    half = HD // 2
    inverse = ROPE_BASE ** (-2.0 * jnp.arange(half, dtype=jnp.float32) / HD)
    angles = places[:, None] * inverse[None, :]
    cosine, sine = jnp.cos(angles), jnp.sin(angles)
    return (
        jnp.concatenate([cosine] * 4, axis=1),
        jnp.concatenate([-sine, sine, -sine, sine], axis=1),
    )

def shifted(count, inner, step):
    return [(a * inner + b, (a + step) % count * inner + b) for a in range(count) for b in range(inner)]


def flipped(count, bit):
    return [(i, i ^ bit) for i in range(count)]


def place_of(count):
    here = lax.axis_index("dp")
    return here // 4, (here // 2) % 2, here % 2, count // 4


def gather_rows(shard, widths):
    count = lax.axis_size("dp")
    if count % 4:
        whole = lax.all_gather(shard, "dp", axis=0, tiled=True)
        ends = [sum(widths[: at + 1]) for at in range(len(widths))]
        return [whole[:, end - each : end] for end, each in zip(ends, widths)]
    outer, pair, core, outers = place_of(count)
    pieces = [(shard, outer, pair)]
    for back in range(1, outers):
        moved = lax.ppermute(shard, "dp", shifted(outers, 4, back))
        pieces.append((moved, (outer - back) % outers, pair))
    for piece, outer_at, _ in list(pieces):
        pieces.append((lax.ppermute(piece, "dp", flipped(count, 2)), outer_at, 1 - pair))
    found, places = [], []
    for piece, outer_at, pair_at in pieces:
        found += [piece, lax.ppermute(piece, "dp", flipped(count, 1))]
        chip = (outer_at * 2 + pair_at) * 2
        places += [chip + core, chip + 1 - core]
    return assemble(found, jnp.stack(places).astype(jnp.int32), widths)


def scatter_rows(partial):
    count = lax.axis_size("dp")
    if count % 4:
        return lax.psum_scatter(partial, "dp", scatter_dimension=0, tiled=True).astype(jnp.float32)
    outer, pair, core, outers = place_of(count)
    held = partial.reshape(outers, 2, 2, partial.shape[0] // count, partial.shape[1])

    def half_sum(values, axis, side, bit):
        kept = lax.dynamic_index_in_dim(values, side, axis, keepdims=False)
        sent = lax.dynamic_index_in_dim(values, 1 - side, axis, keepdims=False)
        got = lax.ppermute(sent, "dp", flipped(count, bit))
        return (kept.astype(jnp.float32) + got.astype(jnp.float32)).astype(values.dtype)

    held = half_sum(held, 2, core, 1)
    held = half_sum(held, 1, pair, 2)
    total = lax.dynamic_index_in_dim(held, outer, 0, keepdims=False).astype(jnp.float32)
    for step in range(1, outers):
        sent = lax.dynamic_index_in_dim(held, (outer + step) % outers, 0, keepdims=False)
        total = total + lax.ppermute(sent, "dp", shifted(outers, 4, step)).astype(jnp.float32)
    return total


def from_pair(rounded):
    if lax.axis_size("mp") != 2:
        total = lax.psum(rounded, "mp").astype(jnp.float32) - rounded.astype(jnp.float32)
        return total.astype(rounded.dtype)
    return lax.ppermute(rounded, "mp", [(0, 1), (1, 0)])


def per_device(tokens, segment_ids, attn_gain, w_qkv, w_out, mlp_gain, w_in, w_ff_out, cotangent):
    count, model = tokens.shape
    shard_rows, width, hidden_here = w_qkv.shape[0], w_qkv.shape[2], w_in.shape[2]
    spare = -hidden_here % LANES
    size = hidden_here + spare
    half, tile = count // 2, count // 4

    def padded(values):
        return jnp.pad(values, ((0, 0), (0, spare)))

    gains = jnp.pad(jnp.stack([attn_gain, mlp_gain], axis=1), ((0, 0), (0, LANES - 2)))
    qkv_w, out_w, gain_columns = gather_rows(
        jnp.concatenate([w_qkv.reshape(shard_rows, -1), w_out.T, gains], axis=1), (3 * width, width, LANES)
    )
    ffn_full = lax.all_gather(
        jnp.concatenate([padded(w_in[:, 0]), padded(w_in[:, 1]), padded(w_ff_out.T)], axis=1),
        "dp",
        axis=0,
        tiled=True,
    )
    gain_one = gain_columns[:, 0].astype(jnp.float32)[None]
    gain_two = gain_columns[:, 1].astype(jnp.float32)[None]

    tables = rope_tables(positions(segment_ids))
    seg_col, seg_row = segment_ids[:, None], segment_ids[None, :]
    resid = tokens.astype(jnp.float32)
    center = resid - jnp.mean(resid, axis=-1, keepdims=True)
    normed_one = center * lax.rsqrt(jnp.mean(center * center, axis=-1, keepdims=True) + EPSILON)
    hidden_one = (normed_one * gain_one).astype(jnp.bfloat16)
    projected = jnp.dot(hidden_one, qkv_w, preferred_element_type=jnp.float32)

    starts = (0, half)
    kept, own, other = (), [], []
    for start in starts:
        *kept, partial = attend(projected, tables, seg_col, seg_row, out_w, start, half, tile, kept)
        own.append(partial)
        other.append(from_pair(partial))
    context, totals = kept

    kept, outs, grads, other_grads, gain_two_grad = (), [], [], [], 0.0
    for at, start in enumerate(starts):
        *kept, out, grad, gain_grad = feed(
            tokens, own[at], other[at], cotangent, gain_two, ffn_full, start, tile, kept
        )
        outs.append(out)
        grads.append(grad)
        other_grads.append(from_pair(grad))
        gain_two_grad = gain_two_grad + gain_grad
    hidden_two, acts = kept
    ffn_total = lax.psum_scatter(
        feed_weights(hidden_two, cotangent, acts, tile), "dp", scatter_dimension=0, tiled=True
    ).astype(jnp.float32)

    kept = ()
    for at, start in enumerate(starts):
        kept = middle_back(
            tokens, own[at], other[at], grads[at], other_grads[at], cotangent, gain_two, out_w, start, tile, kept
        )
    attn_grad_in, context_grad = kept
    outs, _ = lax.optimization_barrier((outs, other_grads[-1]))
    other_outs = [from_pair(out) for out in outs]

    projected_grad = attend_back(projected, tables, seg_col, seg_row, context_grad, context, totals, count)
    out_grad = contract(attn_grad_in, context, 0, 0).astype(jnp.bfloat16)
    one_own, one_other, gain_one_grad = [], [], 0.0
    for start in starts:
        rows = slice(start, start + half)
        partial = sum(
            contract(projected_grad[at, rows], qkv_w[:, at * width : (at + 1) * width], 1, 1) for at in range(3)
        )
        gain_one_grad = gain_one_grad + jnp.sum(partial * normed_one[rows], axis=0)
        one_own.append(partial.astype(jnp.bfloat16))
        one_other.append(from_pair(one_own[-1]))
    gain_grads = jnp.pad(jnp.stack([gain_one_grad, gain_two_grad[0]], axis=1), ((0, 0), (0, LANES - 2)))
    late_total = scatter_rows(jnp.concatenate([out_grad, gain_grads.astype(jnp.bfloat16)], axis=1))
    qkv_total = [
        scatter_rows(contract(hidden_one, projected_grad[at], 0, 0).astype(jnp.bfloat16)) for at in range(3)
    ]
    input_grad = ()
    for at, start in enumerate(starts):
        input_grad = (last(tokens, one_own[at], one_other[at], attn_grad_in, gain_one, start, tile, input_grad),)
    output = jnp.concatenate(
        [
            (
                tokens[start : start + half].astype(jnp.float32)
                + own[at].astype(jnp.float32)
                + other[at].astype(jnp.float32)
                + outs[at].astype(jnp.float32)
                + other_outs[at].astype(jnp.float32)
            ).astype(jnp.bfloat16)
            for at, start in enumerate(starts)
        ]
    )
    gain_total = late_total[:, width : width + 2]
    if lax.axis_size("mp") == 2:
        gain_total = gain_total + lax.ppermute(gain_total, "mp", [(0, 1), (1, 0)])
    else:
        gain_total = lax.psum(gain_total, "mp")
    return (
        output,
        input_grad[0],
        gain_total[:, 0],
        jnp.stack(qkv_total, axis=1),
        late_total[:, :width].T,
        gain_total[:, 1],
        jnp.stack([ffn_total[:, :hidden_here], ffn_total[:, size : size + hidden_here]], axis=1),
        ffn_total[:, 2 * size : 2 * size + hidden_here].T,
    )


def solution(mesh):
    return jax.shard_map(
        per_device,
        mesh=mesh,
        in_specs=(
            P("dp", None),
            P("dp"),
            P("dp"),
            P("dp", None, "mp"),
            P("mp", "dp"),
            P("dp"),
            P("dp", None, "mp"),
            P("mp", "dp"),
            P("dp", None),
        ),
        out_specs=(
            P("dp", None),
            P("dp", None),
            P("dp"),
            P("dp", None, "mp"),
            P("mp", "dp"),
            P("dp"),
            P("dp", None, "mp"),
            P("mp", "dp"),
        ),
        check_vma=False,
    )
```

```python
import functools

import jax
import jax.numpy as jnp
from jax import lax
from jax.experimental import pallas as pl
from jax.experimental.pallas import tpu as pltpu
from jax.sharding import PartitionSpec as P


HD = 64
LANES = 128
EPSILON = 1e-05
ROPE_BASE = 160000.0
NEGATIVE = -1e30
VMEM_BYTES = 60 * 1024 * 1024


def contract(left, right, left_axis, right_axis, **kwargs):
    return lax.dot_general(
        left, right, (((left_axis,), (right_axis,)), ((), ())), preferred_element_type=jnp.float32, **kwargs
    )


def lane_of(rows):
    return lax.broadcasted_iota(jnp.int32, (rows, LANES), 1)


def partner(values):
    front = lane_of(values.shape[0]) % HD < HD // 2
    return jnp.where(
        front, pltpu.roll(values, LANES - HD // 2, 1), pltpu.roll(values, HD // 2, 1)
    )


def rotate(values, cosine, signed_sine):
    return values * cosine + partner(values) * signed_sine


def unrotate(gradient, cosine, signed_sine):
    return gradient * cosine - partner(gradient) * signed_sine


def attend_kernel(
    heads, query_ref, key_ref, value_ref, cos_tile, sin_tile, cos_ref, sin_ref, seg_col, seg_row,
    context_ref, total_ref, keys, values,
):
    score_scale = HD ** (-0.5)

    @pl.when(pl.program_id(0) == 0)
    def _():
        for pair in range(heads // 2):
            cols = slice(pair * LANES, (pair + 1) * LANES)
            keys[:, cols] = rotate(key_ref[:, cols], cos_ref[...], sin_ref[...]).astype(jnp.bfloat16)
        values[...] = value_ref[...].astype(jnp.bfloat16)

    rows = query_ref.shape[0]
    lane = lane_of(rows)
    allowed = seg_col[...] == seg_row[...]
    totals = jnp.zeros((rows, LANES), jnp.float32)
    for pair in range(heads // 2):
        cols = slice(pair * LANES, (pair + 1) * LANES)
        query = rotate(query_ref[:, cols], cos_tile[...], sin_tile[...]) * score_scale
        context = jnp.zeros((rows, LANES), jnp.float32)
        for half in range(2):
            own = lane // HD == half
            scores = contract(jnp.where(own, query, 0.0).astype(jnp.bfloat16), keys[:, cols], 1, 1)
            scores = jnp.where(allowed, scores, NEGATIVE)
            peak = jnp.max(scores, axis=-1, keepdims=True)
            weights = jnp.exp(scores - peak)
            total = jnp.sum(weights, axis=-1, keepdims=True)
            mixed = contract(weights.astype(jnp.bfloat16), values[:, cols], 1, 0)
            context = jnp.where(own, mixed / total, context)
            totals = jnp.where(lane == 2 * pair + half, peak + jnp.log(total), totals)
        context_ref[:, cols] = context.astype(jnp.bfloat16)
    total_ref[...] = totals.T[:heads]


def attend(projected, tables, seg_col, seg_row, start, rows, tile):
    count, width = projected.shape[0], projected.shape[1] // 3
    heads = width // HD
    first = start // tile
    fixed = dict(pipeline_mode=pl.Buffered(1))
    return pl.pallas_call(
        functools.partial(attend_kernel, heads),
        grid=(rows // tile,),
        in_specs=[
            pl.BlockSpec((tile, width), lambda i: (first + i, 0)),
            pl.BlockSpec((count, width), lambda i: (0, 1), **fixed),
            pl.BlockSpec((count, width), lambda i: (0, 2), **fixed),
            pl.BlockSpec((tile, LANES), lambda i: (first + i, 0)),
            pl.BlockSpec((tile, LANES), lambda i: (first + i, 0)),
            pl.BlockSpec((count, LANES), lambda i: (0, 0), **fixed),
            pl.BlockSpec((count, LANES), lambda i: (0, 0), **fixed),
            pl.BlockSpec((tile, 1), lambda i: (first + i, 0)),
            pl.BlockSpec((1, count), lambda i: (0, 0), **fixed),
        ],
        out_specs=[
            pl.BlockSpec((tile, width), lambda i: (i, 0)),
            pl.BlockSpec((heads, tile), lambda i: (0, i)),
        ],
        out_shape=[
            jax.ShapeDtypeStruct((rows, width), jnp.bfloat16),
            jax.ShapeDtypeStruct((heads, rows), jnp.float32),
        ],
        scratch_shapes=[pltpu.VMEM((count, width), jnp.bfloat16), pltpu.VMEM((count, width), jnp.bfloat16)],
        compiler_params=pltpu.CompilerParams(vmem_limit_bytes=VMEM_BYTES),
        cost_estimate=pl.CostEstimate(
            flops=8 * rows * count * width,
            bytes_accessed=4 * count * width * 3 + 2 * rows * width,
            transcendentals=rows * count * heads,
        ),
        name="attend",
    )(projected, projected, projected, *tables, *tables, seg_col, seg_row)


def attend_back_kernel(
    query_ref, key_ref, value_ref, cos_tile, sin_tile, cos_ref, sin_ref, seg_col, seg_row,
    upstream_ref, context_ref, total_ref, *refs, final
):
    score_scale = HD ** (-0.5)
    pair, step = pl.program_id(0), pl.program_id(1)
    query_out, key_out, value_out, keys, values, key_grad, value_grad = refs[-7:]

    @pl.when(step == 0)
    def _():
        keys[...] = rotate(key_ref[...], cos_ref[...], sin_ref[...]).astype(jnp.bfloat16)
        values[...] = value_ref[...].astype(jnp.bfloat16)
        if final:
            key_grad[...] = refs[0][...]
            value_grad[...] = refs[1][...]
        else:
            key_grad[...] = jnp.zeros_like(key_grad)
            value_grad[...] = jnp.zeros_like(value_grad)

    rows = query_ref.shape[0]
    lane = lane_of(rows)
    allowed = seg_col[...] == seg_row[...]
    query = rotate(query_ref[...], cos_tile[...], sin_tile[...]) * score_scale
    upstream = upstream_ref[...].astype(jnp.float32)
    product = upstream * context_ref[...].astype(jnp.float32)
    query_grad = jnp.zeros((rows, LANES), jnp.float32)
    for half in range(2):
        own = lane // HD == half
        own_query = jnp.where(own, query, 0.0).astype(jnp.bfloat16)
        own_upstream = jnp.where(own, upstream, 0.0).astype(jnp.bfloat16)
        picks = (lane_of(8) // HD == half).astype(jnp.float32)
        delta = contract(picks, product, 1, 1, precision=lax.Precision.HIGHEST)[0:1]
        total = total_ref[pl.ds(2 * pair + half, 1), :]
        scores = contract(keys[...], own_query, 1, 1)
        probs = jnp.where(allowed, jnp.exp(scores - total), 0.0)
        prob_grad = contract(values[...], own_upstream, 1, 1)
        score_grad = (probs * (prob_grad - delta)).astype(jnp.bfloat16)
        value_grad[...] += contract(probs.astype(jnp.bfloat16), own_upstream, 1, 0)
        key_grad[...] += contract(score_grad, own_query, 1, 0)
        spread = contract(score_grad, keys[...], 0, 0)
        query_grad = jnp.where(own, spread, query_grad)
    query_out[...] = unrotate(query_grad * score_scale, cos_tile[...], sin_tile[...]).astype(jnp.bfloat16)

    @pl.when(step == pl.num_programs(1) - 1)
    def _():
        if final:
            key_out[...] = unrotate(key_grad[...], cos_ref[...], sin_ref[...]).astype(jnp.bfloat16)
            value_out[...] = value_grad[...].astype(jnp.bfloat16)
        else:
            key_out[...] = key_grad[...]
            value_out[...] = value_grad[...]


def attend_back(projected, tables, seg_col, seg_row, upstream, context, totals, start, tile, final, earlier=()):
    count, width = projected.shape[0], projected.shape[1] // 3
    rows = context.shape[0]
    heads, pairs, first = width // HD, width // LANES, start // tile
    fixed = dict(pipeline_mode=pl.Buffered(1))
    row_block = pl.BlockSpec((tile, LANES), lambda p, i: (i, p))
    whole_block = pl.BlockSpec((count, LANES), lambda p, i: (0, p))
    kind = jnp.bfloat16 if final else jnp.float32
    return pl.pallas_call(
        functools.partial(attend_back_kernel, final=final),
        grid=(pairs, rows // tile),
        in_specs=[
            pl.BlockSpec((tile, LANES), lambda p, i: (first + i, p)),
            pl.BlockSpec((count, LANES), lambda p, i: (0, pairs + p)),
            pl.BlockSpec((count, LANES), lambda p, i: (0, 2 * pairs + p)),
            pl.BlockSpec((tile, LANES), lambda p, i: (first + i, 0)),
            pl.BlockSpec((tile, LANES), lambda p, i: (first + i, 0)),
            pl.BlockSpec((count, LANES), lambda p, i: (0, 0), **fixed),
            pl.BlockSpec((count, LANES), lambda p, i: (0, 0), **fixed),
            pl.BlockSpec((count, 1), lambda p, i: (0, 0), **fixed),
            pl.BlockSpec((1, tile), lambda p, i: (0, first + i)),
            row_block,
            row_block,
            pl.BlockSpec((heads, tile), lambda p, i: (0, i)),
        ]
        + [whole_block] * len(earlier),
        out_specs=[row_block, whole_block, whole_block],
        out_shape=[
            jax.ShapeDtypeStruct((rows, width), jnp.bfloat16),
            jax.ShapeDtypeStruct((count, width), kind),
            jax.ShapeDtypeStruct((count, width), kind),
        ],
        scratch_shapes=[
            pltpu.VMEM((count, LANES), jnp.bfloat16),
            pltpu.VMEM((count, LANES), jnp.bfloat16),
            pltpu.VMEM((count, LANES), jnp.float32),
            pltpu.VMEM((count, LANES), jnp.float32),
        ],
        compiler_params=pltpu.CompilerParams(vmem_limit_bytes=VMEM_BYTES),
        cost_estimate=pl.CostEstimate(
            flops=20 * rows * count * width,
            bytes_accessed=4 * count * width * 3 + 2 * count * width * 5,
            transcendentals=rows * count * heads,
        ),
        name="attend_back",
    )(projected, projected, projected, *tables, *tables, seg_col, seg_row, upstream, context, totals, *earlier)


def feed_kernel(
    tokens_ref, own_ref, other_ref, cot_ref, gain_ref, gate_w, up_w, down_w,
    *refs,
):
    hidden_ref, acts_ref, out_ref, grad_ref, gain_grad_ref = refs[-5:]
    middle = tokens_ref[...].astype(jnp.float32) + (
        own_ref[...].astype(jnp.float32) + other_ref[...].astype(jnp.float32)
    )
    center = middle - jnp.mean(middle, axis=-1, keepdims=True)
    normed = center * lax.rsqrt(jnp.mean(center * center, axis=-1, keepdims=True) + EPSILON)
    hidden = (normed * gain_ref[...]).astype(jnp.bfloat16)
    hidden_ref[...] = hidden
    gate = contract(hidden, gate_w[...], 1, 0)
    upward = contract(hidden, up_w[...], 1, 0)
    mixed_grad = contract(cot_ref[...], down_w[...], 1, 0)
    share = 0.5 * (1.0 + lax.erf(gate * 0.7071067811865476))
    active = gate * share
    slope = share + gate * jnp.exp(-0.5 * gate * gate) * 0.3989422804014327
    size = gate.shape[1]
    gate_grad = (mixed_grad * upward * slope).astype(jnp.bfloat16)
    up_grad = (mixed_grad * active).astype(jnp.bfloat16)
    mixed = (active * upward).astype(jnp.bfloat16)
    acts_ref[:, :size] = gate_grad
    acts_ref[:, size : 2 * size] = up_grad
    acts_ref[:, 2 * size :] = mixed
    out_ref[...] = contract(mixed, down_w[...], 1, 1).astype(jnp.bfloat16)
    partial = contract(gate_grad, gate_w[...], 1, 1) + contract(up_grad, up_w[...], 1, 1)
    grad_ref[...] = partial.astype(jnp.bfloat16)

    @pl.when(pl.program_id(0) == 0)
    def _():
        gain_grad_ref[...] = jnp.zeros_like(gain_grad_ref)

    gain_grad_ref[...] += jnp.sum(partial * normed, axis=0, keepdims=True)


def feed(tokens, own, other, cotangent, gain, ffn_full, start, tile, earlier=()):
    rows, model = own.shape
    size = ffn_full.shape[1] // 3
    first = start // tile
    fixed = dict(pipeline_mode=pl.Buffered(1))
    row_block = pl.BlockSpec((tile, model), lambda i: (i, 0))
    late_block = pl.BlockSpec((tile, model), lambda i: (first + i, 0))
    return pl.pallas_call(
        feed_kernel,
        grid=(rows // tile,),
        in_specs=[
            late_block, row_block, row_block, late_block,
            pl.BlockSpec((1, model), lambda i: (0, 0), **fixed),
            pl.BlockSpec((model, size), lambda i: (0, 0), **fixed),
            pl.BlockSpec((model, size), lambda i: (0, 1), **fixed),
            pl.BlockSpec((model, size), lambda i: (0, 2), **fixed),
        ]
        + [pl.BlockSpec(memory_space=pl.ANY)] * len(earlier),
        out_specs=[
            late_block,
            pl.BlockSpec((tile, 3 * size), lambda i: (first + i, 0)),
            row_block, row_block,
            pl.BlockSpec((1, model), lambda i: (0, 0)),
        ],
        out_shape=[
            jax.ShapeDtypeStruct(tokens.shape, jnp.bfloat16),
            jax.ShapeDtypeStruct((tokens.shape[0], 3 * size), jnp.bfloat16),
            jax.ShapeDtypeStruct((rows, model), jnp.bfloat16),
            jax.ShapeDtypeStruct((rows, model), jnp.bfloat16),
            jax.ShapeDtypeStruct((1, model), jnp.float32),
        ],
        input_output_aliases={8 + at: at for at in range(len(earlier))},
        compiler_params=pltpu.CompilerParams(vmem_limit_bytes=VMEM_BYTES),
        cost_estimate=pl.CostEstimate(
            flops=12 * rows * model * size,
            bytes_accessed=2 * (3 * model * size + 7 * rows * model + 3 * rows * size),
            transcendentals=2 * rows * size,
        ),
        name="feed",
    )(tokens, own, other, cotangent, gain, ffn_full, ffn_full, ffn_full, *earlier)


def norm_of(values):
    center = values - jnp.mean(values, axis=-1, keepdims=True)
    inverse = lax.rsqrt(jnp.mean(center * center, axis=-1, keepdims=True) + EPSILON)
    return center * inverse, inverse


def norm_back(gradient, normed, inverse, gain):
    scaled = gradient * gain
    return inverse * (
        scaled
        - jnp.mean(scaled, axis=-1, keepdims=True)
        - normed * jnp.mean(scaled * normed, axis=-1, keepdims=True)
    )


def project_kernel(count, places_ref, tokens_ref, *refs):
    pieces = refs[:count]
    hidden_ref, projected_ref, weight_ref, gain_ref, columns = refs[count:]
    rows, width = pieces[0].shape[0], weight_ref.shape[1]

    @pl.when(pl.program_id(0) == 0)
    def _():
        for index, piece in enumerate(pieces):
            at = pl.ds(pl.multiple_of(places_ref[index] * rows, rows), rows)
            weight_ref[at, :] = piece[:, :width]
            columns[at, :] = piece[:, width:].astype(jnp.float32)
        gain_ref[...] = columns[...].T[: gain_ref.shape[0]]

    normed, _ = norm_of(tokens_ref[...].astype(jnp.float32))
    hidden = (normed * gain_ref[0:1]).astype(jnp.bfloat16)
    hidden_ref[...] = hidden
    projected_ref[...] = contract(hidden, weight_ref[...], 1, 0)


def project(tokens, pieces, places, tile):
    (count, model), width = tokens.shape, pieces[0].shape[1] - LANES
    fixed = dict(pipeline_mode=pl.Buffered(1))
    return pl.pallas_call(
        functools.partial(project_kernel, len(pieces)),
        grid=(count // tile,),
        in_specs=[pl.BlockSpec(memory_space=pltpu.SMEM), pl.BlockSpec((tile, model), lambda i: (i, 0))]
        + [pl.BlockSpec(piece.shape, lambda i: (0, 0), **fixed) for piece in pieces],
        out_specs=[
            pl.BlockSpec((tile, model), lambda i: (i, 0)),
            pl.BlockSpec((tile, width), lambda i: (i, 0)),
            pl.BlockSpec((model, width), lambda i: (0, 0)),
            pl.BlockSpec((8, model), lambda i: (0, 0)),
        ],
        out_shape=[
            jax.ShapeDtypeStruct((count, model), jnp.bfloat16),
            jax.ShapeDtypeStruct((count, width), jnp.float32),
            jax.ShapeDtypeStruct((model, width), jnp.bfloat16),
            jax.ShapeDtypeStruct((8, model), jnp.float32),
        ],
        scratch_shapes=[pltpu.VMEM((model, LANES), jnp.float32)],
        compiler_params=pltpu.CompilerParams(vmem_limit_bytes=VMEM_BYTES),
        cost_estimate=pl.CostEstimate(
            flops=2 * count * model * width,
            bytes_accessed=4 * count * model + 4 * count * width + 4 * model * width,
            transcendentals=0,
        ),
        name="project",
    )(places, tokens, *pieces)


def assemble_kernel(places_ref, *refs):
    *pieces, out_ref = refs
    rows = pieces[0].shape[0]
    for index, piece in enumerate(pieces):
        out_ref[pl.ds(pl.multiple_of(places_ref[index] * rows, rows), rows), :] = piece[...]


def assemble(pieces, places):
    rows, width = pieces[0].shape
    whole = pl.BlockSpec(memory_space=pltpu.VMEM)
    return pl.pallas_call(
        assemble_kernel,
        in_specs=[pl.BlockSpec(memory_space=pltpu.SMEM)] + [whole] * len(pieces),
        out_specs=whole,
        out_shape=jax.ShapeDtypeStruct((len(pieces) * rows, width), pieces[0].dtype),
        compiler_params=pltpu.CompilerParams(vmem_limit_bytes=VMEM_BYTES),
        cost_estimate=pl.CostEstimate(flops=0, bytes_accessed=4 * len(pieces) * rows * width, transcendentals=0),
        name="assemble",
    )(places, *pieces)


def project_back_kernel(tokens_ref, query_ref, key_ref, value_ref, weight_ref, out_ref, gain_grad_ref):
    width = query_ref.shape[1]
    partial = sum(
        contract(ref[...], weight_ref[:, at * width : (at + 1) * width], 1, 1)
        for at, ref in enumerate((query_ref, key_ref, value_ref))
    )
    out_ref[...] = partial.astype(jnp.bfloat16)
    normed, _ = norm_of(tokens_ref[...].astype(jnp.float32))

    @pl.when(pl.program_id(0) == 0)
    def _():
        gain_grad_ref[...] = jnp.zeros_like(gain_grad_ref)

    gain_grad_ref[...] += jnp.sum(partial * normed, axis=0, keepdims=True)


def project_back(tokens, query_grad, key_grad, value_grad, weight, start, tile):
    rows, width = query_grad.shape
    model, first = tokens.shape[1], start // tile
    late_block = pl.BlockSpec((tile, width), lambda i: (first + i, 0))
    return pl.pallas_call(
        project_back_kernel,
        grid=(rows // tile,),
        in_specs=[
            pl.BlockSpec((tile, model), lambda i: (first + i, 0)),
            pl.BlockSpec((tile, width), lambda i: (i, 0)),
            late_block, late_block,
            pl.BlockSpec(weight.shape, lambda i: (0, 0), pipeline_mode=pl.Buffered(1)),
        ],
        out_specs=[pl.BlockSpec((tile, model), lambda i: (i, 0)), pl.BlockSpec((1, model), lambda i: (0, 0))],
        out_shape=[jax.ShapeDtypeStruct((rows, model), jnp.bfloat16), jax.ShapeDtypeStruct((1, model), jnp.float32)],
        compiler_params=pltpu.CompilerParams(vmem_limit_bytes=VMEM_BYTES),
        cost_estimate=pl.CostEstimate(
            flops=6 * rows * model * width, bytes_accessed=4 * rows * model + 6 * (rows + model) * width,
            transcendentals=0,
        ),
        name="project_back",
    )(tokens, query_grad, key_grad, value_grad, weight)


def middle_back_kernel(
    tokens_ref, own_ref, other_ref, own_grad_ref, other_grad_ref, cot_ref, gain_ref, out_w, grad_ref, context_grad_ref
):
    middle = tokens_ref[...].astype(jnp.float32) + (
        own_ref[...].astype(jnp.float32) + other_ref[...].astype(jnp.float32)
    )
    normed, inverse = norm_of(middle)
    gradient = own_grad_ref[...].astype(jnp.float32) + other_grad_ref[...].astype(jnp.float32)
    back = norm_back(gradient, normed, inverse, gain_ref[...])
    gradient = (cot_ref[...].astype(jnp.float32) + back).astype(jnp.bfloat16)
    grad_ref[...] = gradient
    context_grad_ref[...] = contract(gradient, out_w[...], 1, 0).astype(jnp.bfloat16)


def middle_back(tokens, own, other, own_grad, other_grad, cotangent, gain, out_w, start, tile):
    rows, model = own.shape
    width, first = out_w.shape[1], start // tile
    row_block = pl.BlockSpec((tile, model), lambda i: (i, 0))
    late_block = pl.BlockSpec((tile, model), lambda i: (first + i, 0))
    return pl.pallas_call(
        middle_back_kernel,
        grid=(rows // tile,),
        in_specs=[
            late_block, row_block, row_block, row_block, row_block, late_block,
            pl.BlockSpec((1, model), lambda i: (0, 0)),
            pl.BlockSpec((model, width), lambda i: (0, 0), pipeline_mode=pl.Buffered(1)),
        ],
        out_specs=[row_block, pl.BlockSpec((tile, width), lambda i: (i, 0))],
        out_shape=[jax.ShapeDtypeStruct((rows, model), jnp.bfloat16), jax.ShapeDtypeStruct((rows, width), jnp.bfloat16)],
        compiler_params=pltpu.CompilerParams(vmem_limit_bytes=VMEM_BYTES),
        cost_estimate=pl.CostEstimate(
            flops=2 * rows * model * width, bytes_accessed=2 * (7 * rows * model + model * width), transcendentals=0
        ),
        name="middle_back",
    )(tokens, own, other, own_grad, other_grad, cotangent, gain, out_w)


def last_kernel(tokens_ref, own_grad_ref, other_grad_ref, above_ref, gain_ref, grad_ref):
    normed, inverse = norm_of(tokens_ref[...].astype(jnp.float32))
    gradient = own_grad_ref[...].astype(jnp.float32) + other_grad_ref[...].astype(jnp.float32)
    grad_ref[...] = above_ref[...].astype(jnp.float32) + norm_back(gradient, normed, inverse, gain_ref[...])


def last(tokens, own_grad, other_grad, above, gain, start, tile, earlier=()):
    rows, model = own_grad.shape
    first = start // tile
    row_block = pl.BlockSpec((tile, model), lambda i: (i, 0))
    late_block = pl.BlockSpec((tile, model), lambda i: (first + i, 0))

    def body(*refs):
        last_kernel(*refs[:5], refs[-1])

    return pl.pallas_call(
        body,
        grid=(rows // tile,),
        in_specs=[late_block, row_block, row_block, row_block, pl.BlockSpec((1, model), lambda i: (0, 0))]
        + [pl.BlockSpec(memory_space=pl.ANY)] * len(earlier),
        out_specs=late_block,
        out_shape=jax.ShapeDtypeStruct(tokens.shape, jnp.float32),
        input_output_aliases={5 + at: at for at in range(len(earlier))},
        compiler_params=pltpu.CompilerParams(vmem_limit_bytes=VMEM_BYTES),
        cost_estimate=pl.CostEstimate(flops=20 * rows * model, bytes_accessed=12 * rows * model, transcendentals=0),
        name="last",
    )(tokens, own_grad, other_grad, above, gain, *earlier)


def feed_weights_kernel(hidden_ref, cot_ref, acts_ref, out_ref):
    @pl.when(pl.program_id(0) < 2)
    def _():
        out_ref[...] = contract(hidden_ref[...], acts_ref[...], 0, 0).astype(jnp.bfloat16)

    @pl.when(pl.program_id(0) == 2)
    def _():
        out_ref[...] = contract(cot_ref[...], acts_ref[...], 0, 0).astype(jnp.bfloat16)


def feed_weights(hidden, cotangent, acts, tile):
    count, model = hidden.shape
    size = acts.shape[1] // 3
    return pl.pallas_call(
        feed_weights_kernel,
        grid=(3, model // tile),
        in_specs=[
            pl.BlockSpec((count, tile), lambda j, i: (0, i)),
            pl.BlockSpec((count, tile), lambda j, i: (0, i)),
            pl.BlockSpec((count, size), lambda j, i: (0, j)),
        ],
        out_specs=pl.BlockSpec((tile, size), lambda j, i: (i, j)),
        out_shape=jax.ShapeDtypeStruct((model, 3 * size), jnp.bfloat16),
        compiler_params=pltpu.CompilerParams(vmem_limit_bytes=VMEM_BYTES),
        cost_estimate=pl.CostEstimate(
            flops=6 * count * model * size, bytes_accessed=6 * count * size + 4 * count * model + 6 * model * size,
            transcendentals=0,
        ),
        name="feed_weights",
    )(hidden, cotangent, acts)


def positions(segment_ids):
    index_row = jnp.arange(segment_ids.shape[0], dtype=jnp.int32)
    change = jnp.concatenate([jnp.ones((1,), bool), segment_ids[1:] != segment_ids[:-1]])
    marker = jnp.where(change, index_row, jnp.zeros_like(index_row))
    starts = lax.cummax(marker, axis=0)
    return (index_row - starts).astype(jnp.float32)


def rope_tables(places):
    half = HD // 2
    inverse = ROPE_BASE ** (-2.0 * jnp.arange(half, dtype=jnp.float32) / HD)
    angles = places[:, None] * inverse[None, :]
    cosine, sine = jnp.cos(angles), jnp.sin(angles)
    return (
        jnp.concatenate([cosine] * 4, axis=1),
        jnp.concatenate([-sine, sine, -sine, sine], axis=1),
    )


def shifted(count, inner, step):
    return [(a * inner + b, (a + step) % count * inner + b) for a in range(count) for b in range(inner)]


def flipped(count, bit):
    return [(i, i ^ bit) for i in range(count)]


def place_of(count):
    here = lax.axis_index("dp")
    return here // 4, (here // 2) % 2, here % 2, count // 4


def gather_pieces(shard, after=None):
    count = lax.axis_size("dp")
    if count % 4:
        return [lax.all_gather(shard, "dp", axis=0, tiled=True)], jnp.zeros((1,), jnp.int32), shard
    if after is not None:
        shard, _ = lax.optimization_barrier((shard, after))
    outer, pair, core, outers = place_of(count)
    pieces = [(shard, outer, pair)]
    for back in range(1, outers):
        moved = lax.ppermute(shard, "dp", shifted(outers, 4, back))
        pieces.append((moved, (outer - back) % outers, pair))
    arrived = [piece for piece, _, _ in pieces]
    for piece, outer_at, _ in list(pieces):
        pieces.append((lax.ppermute(piece, "dp", flipped(count, 2)), outer_at, 1 - pair))
    found, places = [], []
    for piece, outer_at, pair_at in pieces:
        found += [piece, lax.ppermute(piece, "dp", flipped(count, 1))]
        chip = (outer_at * 2 + pair_at) * 2
        places += [chip + core, chip + 1 - core]
    return found, jnp.stack(places).astype(jnp.int32), arrived


def scatter_rows(partial):
    count = lax.axis_size("dp")
    if count % 4:
        return lax.psum_scatter(partial, "dp", scatter_dimension=0, tiled=True).astype(jnp.float32)
    outer, pair, core, outers = place_of(count)
    held = partial.reshape(outers, 2, 2, partial.shape[0] // count, partial.shape[1])

    def half_sum(values, axis, side, bit):
        kept = lax.dynamic_index_in_dim(values, side, axis, keepdims=False)
        sent = lax.dynamic_index_in_dim(values, 1 - side, axis, keepdims=False)
        got = lax.ppermute(sent, "dp", flipped(count, bit))
        return (kept.astype(jnp.float32) + got.astype(jnp.float32)).astype(values.dtype)

    held = half_sum(held, 2, core, 1)
    held = half_sum(held, 1, pair, 2)
    total = lax.dynamic_index_in_dim(held, outer, 0, keepdims=False).astype(jnp.float32)
    for step in range(1, outers):
        sent = lax.dynamic_index_in_dim(held, (outer + step) % outers, 0, keepdims=False)
        total = total + lax.ppermute(sent, "dp", shifted(outers, 4, step)).astype(jnp.float32)
    return total


def from_pair(rounded):
    if lax.axis_size("mp") != 2:
        total = lax.psum(rounded, "mp").astype(jnp.float32) - rounded.astype(jnp.float32)
        return total.astype(rounded.dtype)
    return lax.ppermute(rounded, "mp", [(0, 1), (1, 0)])


def layer(tokens, segment_ids, attn_gain, w_qkv, w_out, mlp_gain, w_in, w_ff_out, cotangent):
    count, _ = tokens.shape
    shard_rows, hidden_here = w_qkv.shape[0], w_in.shape[2]
    spare = -hidden_here % LANES
    size = hidden_here + spare
    half, tile = count // 2, count // 4
    starts = (0, half)

    def padded(values):
        return jnp.pad(values, ((0, 0), (0, spare)))

    gains = jnp.pad(jnp.stack([attn_gain, mlp_gain], axis=1), ((0, 0), (0, LANES - 2)))
    pieces, places, arrived = gather_pieces(jnp.concatenate([w_qkv.reshape(shard_rows, -1), gains], axis=1))
    out_pieces, out_places, _ = gather_pieces(w_out.T, arrived)
    ffn_full = lax.all_gather(
        jnp.concatenate([padded(w_in[:, 0]), padded(w_in[:, 1]), padded(w_ff_out.T)], axis=1),
        "dp",
        axis=0,
        tiled=True,
    )
    tables = rope_tables(positions(segment_ids))
    seg_col, seg_row = segment_ids[:, None], segment_ids[None, :]
    hidden_one, projected, qkv_w, gain_rows = project(tokens, pieces, places, tile)
    gain_one, gain_two = gain_rows[0:1], gain_rows[1:2]
    out_w = assemble(out_pieces, out_places)

    contexts, totals, own, other = [], [], [], []
    for start in starts:
        context, total = attend(projected, tables, seg_col, seg_row, start, half, tile)
        contexts.append(context)
        totals.append(total)
        own.append(contract(context, out_w, 1, 1).astype(jnp.bfloat16))
        other.append(from_pair(own[-1]))

    kept, outs, grads, other_grads, gain_two_grad = (), [], [], [], 0.0
    for at, start in enumerate(starts):
        *kept, out, grad, gain_grad = feed(tokens, own[at], other[at], cotangent, gain_two, ffn_full, start, tile, kept)
        outs.append(out)
        grads.append(grad)
        other_grads.append(from_pair(grad))
        gain_two_grad = gain_two_grad + gain_grad
    hidden_two, acts = kept
    feed_grads = feed_weights(hidden_two, cotangent, acts, tile)
    ffn_total = lax.psum_scatter(feed_grads, "dp", scatter_dimension=0, tiled=True).astype(jnp.float32)

    attn_grad_in, query_grads, sums = [], [], ()
    for at, start in enumerate(starts):
        gradient, context_grad = middle_back(
            tokens, own[at], other[at], grads[at], other_grads[at], cotangent, gain_two, out_w, start, tile
        )
        attn_grad_in.append(gradient)
        query_grad, *sums = attend_back(
            projected, tables, seg_col, seg_row, context_grad, contexts[at], totals[at], start, half,
            at == len(starts) - 1, sums,
        )
        query_grads.append(query_grad)
    outs, _ = lax.optimization_barrier((outs, other_grads[-1]))
    other_outs = []
    for out in outs:
        other_outs.append(from_pair(out))
    out_grad = sum(contract(attn_grad_in[at], contexts[at], 0, 0) for at in range(len(starts))).astype(jnp.bfloat16)
    key_grad, value_grad = sums
    one_own, one_other, gain_one_grad = [], [], 0.0
    for at, start in enumerate(starts):
        partial, gain_grad = project_back(tokens, query_grads[at], key_grad, value_grad, qkv_w, start, tile)
        gain_one_grad = gain_one_grad + gain_grad
        one_own.append(partial)
        one_other.append(from_pair(partial))
    out_total = scatter_rows(out_grad)
    qkv_total = [
        scatter_rows(contract(hidden_one, jnp.concatenate(query_grads), 0, 0).astype(jnp.bfloat16)),
        scatter_rows(contract(hidden_one, key_grad, 0, 0).astype(jnp.bfloat16)),
        scatter_rows(contract(hidden_one, value_grad, 0, 0).astype(jnp.bfloat16)),
    ]
    gain_grads = jnp.pad(jnp.concatenate([gain_one_grad, gain_two_grad]).T, ((0, 0), (0, LANES - 2)))
    gain_total = scatter_rows(gain_grads)[:, :2]
    if lax.axis_size("mp") == 2:
        gain_total = gain_total + lax.ppermute(gain_total, "mp", [(0, 1), (1, 0)])
    else:
        gain_total = lax.psum(gain_total, "mp")
    input_grad = ()
    for at, start in enumerate(starts):
        input_grad = (
            last(tokens, one_own[at], one_other[at], attn_grad_in[at], gain_one, start, tile, input_grad),
        )
    output = jnp.concatenate(
        [
            (
                tokens[start : start + half].astype(jnp.float32)
                + own[at].astype(jnp.float32)
                + other[at].astype(jnp.float32)
                + outs[at].astype(jnp.float32)
                + other_outs[at].astype(jnp.float32)
            ).astype(jnp.bfloat16)
            for at, start in enumerate(starts)
        ]
    )
    return (
        output,
        input_grad[0],
        gain_total[:, 0],
        jnp.stack(qkv_total, axis=1),
        out_total.T,
        gain_total[:, 1],
        jnp.stack([ffn_total[:, :hidden_here], ffn_total[:, size : size + hidden_here]], axis=1),
        ffn_total[:, 2 * size : 2 * size + hidden_here].T,
    )


def solution(mesh):
    return jax.shard_map(
        layer,
        mesh=mesh,
        in_specs=(
            P("dp", None),
            P("dp"),
            P("dp"),
            P("dp", None, "mp"),
            P("mp", "dp"),
            P("dp"),
            P("dp", None, "mp"),
            P("mp", "dp"),
            P("dp", None),
        ),
        out_specs=(
            P("dp", None),
            P("dp", None),
            P("dp"),
            P("dp", None, "mp"),
            P("mp", "dp"),
            P("dp"),
            P("dp", None, "mp"),
            P("mp", "dp"),
        ),
        check_vma=False,
    )
```

```python
import functools

import jax
import jax.numpy as jnp
from jax import lax
from jax.experimental import pallas as pl
from jax.experimental.pallas import tpu as pltpu
from jax.sharding import PartitionSpec as P


HD = 64
LANES = 128
EPSILON = 1e-05
ROPE_BASE = 160000.0
NEGATIVE = -1e30
VMEM_BYTES = 60 * 1024 * 1024


def contract(left, right, left_axis, right_axis, **kwargs):
    return lax.dot_general(
        left, right, (((left_axis,), (right_axis,)), ((), ())), preferred_element_type=jnp.float32, **kwargs
    )


def lane_of(rows):
    return lax.broadcasted_iota(jnp.int32, (rows, LANES), 1)


def partner(values):
    front = lane_of(values.shape[0]) % HD < HD // 2
    return jnp.where(
        front, pltpu.roll(values, LANES - HD // 2, 1), pltpu.roll(values, HD // 2, 1)
    )


def rotate(values, cosine, signed_sine):
    return values * cosine + partner(values) * signed_sine


def unrotate(gradient, cosine, signed_sine):
    return gradient * cosine - partner(gradient) * signed_sine


def attend_kernel(
    heads, query_ref, key_ref, value_ref, cos_tile, sin_tile, cos_ref, sin_ref, seg_col, seg_row,
    *refs,
):
    context_ref, whole_ref, total_ref, keys, values = refs[-5:]
    score_scale = HD ** (-0.5)

    @pl.when(pl.program_id(0) == 0)
    def _():
        for pair in range(heads // 2):
            cols = slice(pair * LANES, (pair + 1) * LANES)
            keys[:, cols] = rotate(key_ref[:, cols], cos_ref[...], sin_ref[...]).astype(jnp.bfloat16)
        values[...] = value_ref[...].astype(jnp.bfloat16)

    rows = query_ref.shape[0]
    lane = lane_of(rows)
    allowed = seg_col[...] == seg_row[...]
    totals = jnp.zeros((rows, LANES), jnp.float32)
    for pair in range(heads // 2):
        cols = slice(pair * LANES, (pair + 1) * LANES)
        query = rotate(query_ref[:, cols], cos_tile[...], sin_tile[...]) * score_scale
        context = jnp.zeros((rows, LANES), jnp.float32)
        for half in range(2):
            own = lane // HD == half
            scores = contract(jnp.where(own, query, 0.0).astype(jnp.bfloat16), keys[:, cols], 1, 1)
            scores = jnp.where(allowed, scores, NEGATIVE)
            peak = jnp.max(scores, axis=-1, keepdims=True)
            weights = jnp.exp(scores - peak)
            total = jnp.sum(weights, axis=-1, keepdims=True)
            mixed = contract(weights.astype(jnp.bfloat16), values[:, cols], 1, 0)
            context = jnp.where(own, mixed / total, context)
            totals = jnp.where(lane == 2 * pair + half, peak + jnp.log(total), totals)
        context_ref[:, cols] = context.astype(jnp.bfloat16)
        whole_ref[:, cols] = context.astype(jnp.bfloat16)
    total_ref[...] = totals.T[:heads]


def attend(projected, tables, seg_col, seg_row, start, rows, tile, earlier=()):
    count, width = projected.shape[0], projected.shape[1] // 3
    heads = width // HD
    first = start // tile
    fixed = dict(pipeline_mode=pl.Buffered(1))
    return pl.pallas_call(
        functools.partial(attend_kernel, heads),
        grid=(rows // tile,),
        in_specs=[
            pl.BlockSpec((tile, width), lambda i: (first + i, 0)),
            pl.BlockSpec((count, width), lambda i: (0, 1), **fixed),
            pl.BlockSpec((count, width), lambda i: (0, 2), **fixed),
            pl.BlockSpec((tile, LANES), lambda i: (first + i, 0)),
            pl.BlockSpec((tile, LANES), lambda i: (first + i, 0)),
            pl.BlockSpec((count, LANES), lambda i: (0, 0), **fixed),
            pl.BlockSpec((count, LANES), lambda i: (0, 0), **fixed),
            pl.BlockSpec((tile, 1), lambda i: (first + i, 0)),
            pl.BlockSpec((1, count), lambda i: (0, 0), **fixed),
        ]
        + [pl.BlockSpec(memory_space=pl.ANY)] * len(earlier),
        out_specs=[
            pl.BlockSpec((tile, width), lambda i: (i, 0)),
            pl.BlockSpec((tile, width), lambda i: (first + i, 0)),
            pl.BlockSpec((heads, tile), lambda i: (0, first + i)),
        ],
        out_shape=[
            jax.ShapeDtypeStruct((rows, width), jnp.bfloat16),
            jax.ShapeDtypeStruct((count, width), jnp.bfloat16),
            jax.ShapeDtypeStruct((heads, count), jnp.float32),
        ],
        input_output_aliases={9 + at: 1 + at for at in range(len(earlier))},
        scratch_shapes=[pltpu.VMEM((count, width), jnp.bfloat16), pltpu.VMEM((count, width), jnp.bfloat16)],
        compiler_params=pltpu.CompilerParams(vmem_limit_bytes=VMEM_BYTES),
        cost_estimate=pl.CostEstimate(
            flops=8 * rows * count * width,
            bytes_accessed=4 * count * width * 3 + 2 * rows * width,
            transcendentals=rows * count * heads,
        ),
        name="attend",
    )(projected, projected, projected, *tables, *tables, seg_col, seg_row, *earlier)


def attend_back_kernel(
    query_ref, key_ref, value_ref, cos_tile, sin_tile, cos_ref, sin_ref, seg_col, seg_row,
    upstream_ref, context_ref, total_ref, query_out, key_out, value_out, keys, values, key_grad, value_grad, *, first
):
    score_scale = HD ** (-0.5)
    pair, step = first + pl.program_id(0), pl.program_id(1)

    @pl.when(step == 0)
    def _():
        keys[...] = rotate(key_ref[...], cos_ref[...], sin_ref[...]).astype(jnp.bfloat16)
        values[...] = value_ref[...].astype(jnp.bfloat16)
        key_grad[...] = jnp.zeros_like(key_grad)
        value_grad[...] = jnp.zeros_like(value_grad)

    rows = query_ref.shape[0]
    lane = lane_of(rows)
    allowed = seg_col[...] == seg_row[...]
    query = rotate(query_ref[...], cos_tile[...], sin_tile[...]) * score_scale
    upstream = upstream_ref[...].astype(jnp.float32)
    product = upstream * context_ref[...].astype(jnp.float32)
    query_grad = jnp.zeros((rows, LANES), jnp.float32)
    for half in range(2):
        own = lane // HD == half
        own_query = jnp.where(own, query, 0.0).astype(jnp.bfloat16)
        own_upstream = jnp.where(own, upstream, 0.0).astype(jnp.bfloat16)
        picks = (lane_of(8) // HD == half).astype(jnp.float32)
        delta = contract(picks, product, 1, 1, precision=lax.Precision.HIGHEST)[0:1]
        total = total_ref[pl.ds(2 * pair + half, 1), :]
        scores = contract(keys[...], own_query, 1, 1)
        probs = jnp.where(allowed, jnp.exp(scores - total), 0.0)
        prob_grad = contract(values[...], own_upstream, 1, 1)
        score_grad = (probs * (prob_grad - delta)).astype(jnp.bfloat16)
        value_grad[...] += contract(probs.astype(jnp.bfloat16), own_upstream, 1, 0)
        key_grad[...] += contract(score_grad, own_query, 1, 0)
        spread = contract(score_grad, keys[...], 0, 0)
        query_grad = jnp.where(own, spread, query_grad)
    query_out[...] = unrotate(query_grad * score_scale, cos_tile[...], sin_tile[...]).astype(jnp.bfloat16)

    @pl.when(step == pl.num_programs(1) - 1)
    def _():
        key_out[...] = unrotate(key_grad[...], cos_ref[...], sin_ref[...]).astype(jnp.bfloat16)
        value_out[...] = value_grad[...].astype(jnp.bfloat16)


def attend_back(projected, tables, seg_col, seg_row, upstream, context, totals, first, taken, tile):
    count, width = projected.shape[0], projected.shape[1] // 3
    heads, pairs = width // HD, width // LANES
    fixed = dict(pipeline_mode=pl.Buffered(1))
    row_block = pl.BlockSpec((tile, LANES), lambda p, i: (i, first + p))
    whole_block = pl.BlockSpec((count, LANES), lambda p, i: (0, p))
    return pl.pallas_call(
        functools.partial(attend_back_kernel, first=first),
        grid=(taken, count // tile),
        in_specs=[
            row_block,
            pl.BlockSpec((count, LANES), lambda p, i: (0, pairs + first + p)),
            pl.BlockSpec((count, LANES), lambda p, i: (0, 2 * pairs + first + p)),
            pl.BlockSpec((tile, LANES), lambda p, i: (i, 0)),
            pl.BlockSpec((tile, LANES), lambda p, i: (i, 0)),
            pl.BlockSpec((count, LANES), lambda p, i: (0, 0), **fixed),
            pl.BlockSpec((count, LANES), lambda p, i: (0, 0), **fixed),
            pl.BlockSpec((count, 1), lambda p, i: (0, 0), **fixed),
            pl.BlockSpec((1, tile), lambda p, i: (0, i)),
            row_block,
            row_block,
            pl.BlockSpec((heads, tile), lambda p, i: (0, i)),
        ],
        out_specs=[pl.BlockSpec((tile, LANES), lambda p, i: (i, p)), whole_block, whole_block],
        out_shape=[jax.ShapeDtypeStruct((count, taken * LANES), jnp.bfloat16)] * 3,
        scratch_shapes=[
            pltpu.VMEM((count, LANES), jnp.bfloat16),
            pltpu.VMEM((count, LANES), jnp.bfloat16),
            pltpu.VMEM((count, LANES), jnp.float32),
            pltpu.VMEM((count, LANES), jnp.float32),
        ],
        compiler_params=pltpu.CompilerParams(vmem_limit_bytes=VMEM_BYTES),
        cost_estimate=pl.CostEstimate(
            flops=20 * count * count * taken * LANES,
            bytes_accessed=22 * count * taken * LANES,
            transcendentals=2 * count * count * taken,
        ),
        name="attend_back",
    )(projected, projected, projected, *tables, *tables, seg_col, seg_row, upstream, context, totals)


def feed_kernel(
    tokens_ref, own_ref, other_ref, cot_ref, gain_ref, gate_w, up_w, down_w,
    *refs,
):
    hidden_ref, acts_ref, out_ref, grad_ref, gain_grad_ref = refs[-5:]
    middle = tokens_ref[...].astype(jnp.float32) + (
        own_ref[...].astype(jnp.float32) + other_ref[...].astype(jnp.float32)
    )
    center = middle - jnp.mean(middle, axis=-1, keepdims=True)
    normed = center * lax.rsqrt(jnp.mean(center * center, axis=-1, keepdims=True) + EPSILON)
    hidden = (normed * gain_ref[...]).astype(jnp.bfloat16)
    hidden_ref[...] = hidden
    gate = contract(hidden, gate_w[...], 1, 0)
    upward = contract(hidden, up_w[...], 1, 0)
    mixed_grad = contract(cot_ref[...], down_w[...], 1, 0)
    share = 0.5 * (1.0 + lax.erf(gate * 0.7071067811865476))
    active = gate * share
    slope = share + gate * jnp.exp(-0.5 * gate * gate) * 0.3989422804014327
    size = gate.shape[1]
    gate_grad = (mixed_grad * upward * slope).astype(jnp.bfloat16)
    up_grad = (mixed_grad * active).astype(jnp.bfloat16)
    mixed = (active * upward).astype(jnp.bfloat16)
    acts_ref[:, :size] = gate_grad
    acts_ref[:, size : 2 * size] = up_grad
    acts_ref[:, 2 * size :] = mixed
    out_ref[...] = contract(mixed, down_w[...], 1, 1).astype(jnp.bfloat16)
    partial = contract(gate_grad, gate_w[...], 1, 1) + contract(up_grad, up_w[...], 1, 1)
    grad_ref[...] = partial.astype(jnp.bfloat16)

    @pl.when(pl.program_id(0) == 0)
    def _():
        gain_grad_ref[...] = jnp.zeros_like(gain_grad_ref)

    gain_grad_ref[...] += jnp.sum(partial * normed, axis=0, keepdims=True)


def feed(tokens, own, other, cotangent, gain, ffn_full, start, tile, earlier=()):
    rows, model = own.shape
    size = ffn_full.shape[1] // 3
    first = start // tile
    fixed = dict(pipeline_mode=pl.Buffered(1))
    row_block = pl.BlockSpec((tile, model), lambda i: (i, 0))
    late_block = pl.BlockSpec((tile, model), lambda i: (first + i, 0))
    return pl.pallas_call(
        feed_kernel,
        grid=(rows // tile,),
        in_specs=[
            late_block, row_block, row_block, late_block,
            pl.BlockSpec((1, model), lambda i: (0, 0), **fixed),
            pl.BlockSpec((model, size), lambda i: (0, 0), **fixed),
            pl.BlockSpec((model, size), lambda i: (0, 1), **fixed),
            pl.BlockSpec((model, size), lambda i: (0, 2), **fixed),
        ]
        + [pl.BlockSpec(memory_space=pl.ANY)] * len(earlier),
        out_specs=[
            late_block,
            pl.BlockSpec((tile, 3 * size), lambda i: (first + i, 0)),
            row_block, row_block,
            pl.BlockSpec((1, model), lambda i: (0, 0)),
        ],
        out_shape=[
            jax.ShapeDtypeStruct(tokens.shape, jnp.bfloat16),
            jax.ShapeDtypeStruct((tokens.shape[0], 3 * size), jnp.bfloat16),
            jax.ShapeDtypeStruct((rows, model), jnp.bfloat16),
            jax.ShapeDtypeStruct((rows, model), jnp.bfloat16),
            jax.ShapeDtypeStruct((1, model), jnp.float32),
        ],
        input_output_aliases={8 + at: at for at in range(len(earlier))},
        compiler_params=pltpu.CompilerParams(vmem_limit_bytes=VMEM_BYTES),
        cost_estimate=pl.CostEstimate(
            flops=12 * rows * model * size,
            bytes_accessed=2 * (3 * model * size + 7 * rows * model + 3 * rows * size),
            transcendentals=2 * rows * size,
        ),
        name="feed",
    )(tokens, own, other, cotangent, gain, ffn_full, ffn_full, ffn_full, *earlier)


def norm_of(values):
    center = values - jnp.mean(values, axis=-1, keepdims=True)
    inverse = lax.rsqrt(jnp.mean(center * center, axis=-1, keepdims=True) + EPSILON)
    return center * inverse, inverse


def norm_back(gradient, normed, inverse, gain):
    scaled = gradient * gain
    return inverse * (
        scaled
        - jnp.mean(scaled, axis=-1, keepdims=True)
        - normed * jnp.mean(scaled * normed, axis=-1, keepdims=True)
    )


def project_kernel(count, places_ref, tokens_ref, *refs):
    pieces = refs[:count]
    hidden_ref, projected_ref, weight_ref, gain_ref, columns = refs[count:]
    rows, width = pieces[0].shape[0], weight_ref.shape[1]

    @pl.when(pl.program_id(0) == 0)
    def _():
        for index, piece in enumerate(pieces):
            at = pl.ds(pl.multiple_of(places_ref[index] * rows, rows), rows)
            weight_ref[at, :] = piece[:, :width]
            columns[at, :] = piece[:, width:].astype(jnp.float32)
        gain_ref[...] = columns[...].T[: gain_ref.shape[0]]

    normed, _ = norm_of(tokens_ref[...].astype(jnp.float32))
    hidden = (normed * gain_ref[0:1]).astype(jnp.bfloat16)
    hidden_ref[...] = hidden
    projected_ref[...] = contract(hidden, weight_ref[...], 1, 0)


def project(tokens, pieces, places, tile):
    (count, model), width = tokens.shape, pieces[0].shape[1] - LANES
    fixed = dict(pipeline_mode=pl.Buffered(1))
    return pl.pallas_call(
        functools.partial(project_kernel, len(pieces)),
        grid=(count // tile,),
        in_specs=[pl.BlockSpec(memory_space=pltpu.SMEM), pl.BlockSpec((tile, model), lambda i: (i, 0))]
        + [pl.BlockSpec(piece.shape, lambda i: (0, 0), **fixed) for piece in pieces],
        out_specs=[
            pl.BlockSpec((tile, model), lambda i: (i, 0)),
            pl.BlockSpec((tile, width), lambda i: (i, 0)),
            pl.BlockSpec((model, width), lambda i: (0, 0)),
            pl.BlockSpec((8, model), lambda i: (0, 0)),
        ],
        out_shape=[
            jax.ShapeDtypeStruct((count, model), jnp.bfloat16),
            jax.ShapeDtypeStruct((count, width), jnp.float32),
            jax.ShapeDtypeStruct((model, width), jnp.bfloat16),
            jax.ShapeDtypeStruct((8, model), jnp.float32),
        ],
        scratch_shapes=[pltpu.VMEM((model, LANES), jnp.float32)],
        compiler_params=pltpu.CompilerParams(vmem_limit_bytes=VMEM_BYTES),
        cost_estimate=pl.CostEstimate(
            flops=2 * count * model * width,
            bytes_accessed=4 * count * model + 4 * count * width + 4 * model * width,
            transcendentals=0,
        ),
        name="project",
    )(places, tokens, *pieces)


def assemble_kernel(places_ref, *refs):
    *pieces, out_ref = refs
    rows = pieces[0].shape[0]
    for index, piece in enumerate(pieces):
        out_ref[pl.ds(pl.multiple_of(places_ref[index] * rows, rows), rows), :] = piece[...]


def assemble(pieces, places):
    rows, width = pieces[0].shape
    whole = pl.BlockSpec(memory_space=pltpu.VMEM)
    return pl.pallas_call(
        assemble_kernel,
        in_specs=[pl.BlockSpec(memory_space=pltpu.SMEM)] + [whole] * len(pieces),
        out_specs=whole,
        out_shape=jax.ShapeDtypeStruct((len(pieces) * rows, width), pieces[0].dtype),
        compiler_params=pltpu.CompilerParams(vmem_limit_bytes=VMEM_BYTES),
        cost_estimate=pl.CostEstimate(flops=0, bytes_accessed=4 * len(pieces) * rows * width, transcendentals=0),
        name="assemble",
    )(places, *pieces)


def project_back_kernel(groups, tokens_ref, weight_ref, *refs):
    grads, (out_ref, gain_grad_ref) = refs[: 3 * groups], refs[3 * groups :]
    size = grads[0].shape[1]
    partial = 0.0
    for at, ref in enumerate(grads):
        begin = (at % 3 * groups + at // 3) * size
        partial = partial + contract(ref[...], weight_ref[:, begin : begin + size], 1, 1)
    out_ref[...] = partial.astype(jnp.bfloat16)
    normed, _ = norm_of(tokens_ref[...].astype(jnp.float32))

    @pl.when(pl.program_id(0) == 0)
    def _():
        gain_grad_ref[...] = jnp.zeros_like(gain_grad_ref)

    gain_grad_ref[...] += jnp.sum(partial * normed, axis=0, keepdims=True)


def project_back(tokens, grads, weight, start, rows, tile):
    model, first = tokens.shape[1], start // tile
    late = lambda i: (first + i, 0)
    return pl.pallas_call(
        functools.partial(project_back_kernel, len(grads) // 3),
        grid=(rows // tile,),
        in_specs=[
            pl.BlockSpec((tile, model), late),
            pl.BlockSpec(weight.shape, lambda i: (0, 0), pipeline_mode=pl.Buffered(1)),
        ]
        + [pl.BlockSpec((tile, grad.shape[1]), late) for grad in grads],
        out_specs=[pl.BlockSpec((tile, model), lambda i: (i, 0)), pl.BlockSpec((1, model), lambda i: (0, 0))],
        out_shape=[jax.ShapeDtypeStruct((rows, model), jnp.bfloat16), jax.ShapeDtypeStruct((1, model), jnp.float32)],
        compiler_params=pltpu.CompilerParams(vmem_limit_bytes=VMEM_BYTES),
        cost_estimate=pl.CostEstimate(
            flops=2 * rows * model * weight.shape[1],
            bytes_accessed=4 * rows * model + 2 * (rows + model) * weight.shape[1],
            transcendentals=0,
        ),
        name="project_back",
    )(tokens, weight, *grads)


def parted_weights_kernel(core_ref, left_ref, *refs):
    *rights, kept_ref, sent_ref = refs
    product = jnp.concatenate([contract(left_ref[...], right[...], 0, 0) for right in rights], axis=1)
    product = product.astype(jnp.bfloat16)
    rows = product.shape[0] // 4
    first_core = core_ref[0] == 0
    for pair in range(2):
        even = product[2 * pair * rows : (2 * pair + 1) * rows]
        odd = product[(2 * pair + 1) * rows : (2 * pair + 2) * rows]
        at = slice(pair * rows, (pair + 1) * rows)
        kept_ref[at] = jnp.where(first_core, even, odd)
        sent_ref[at] = jnp.where(first_core, odd, even)


def parted_weights(left, rights, core, outers):
    count, model = left.shape
    width = sum(right.shape[1] for right in rights)
    tile = model // outers
    half_block = pl.BlockSpec((tile // 2, width), lambda i: (i, 0))
    return pl.pallas_call(
        parted_weights_kernel,
        grid=(outers,),
        in_specs=[pl.BlockSpec(memory_space=pltpu.SMEM), pl.BlockSpec((count, tile), lambda i: (0, i))]
        + [pl.BlockSpec(right.shape, lambda i: (0, 0), pipeline_mode=pl.Buffered(1)) for right in rights],
        out_specs=[half_block, half_block],
        out_shape=[jax.ShapeDtypeStruct((model // 2, width), jnp.bfloat16)] * 2,
        compiler_params=pltpu.CompilerParams(vmem_limit_bytes=VMEM_BYTES),
        cost_estimate=pl.CostEstimate(
            flops=2 * count * model * width, bytes_accessed=2 * (count + model) * width + 2 * count * model,
            transcendentals=0,
        ),
        name="parted_weights",
    )(core, left, *rights)


def middle_back_kernel(
    tokens_ref, own_ref, other_ref, own_grad_ref, other_grad_ref, cot_ref, gain_ref, out_w, *refs
):
    grad_ref, context_grad_ref = refs[-2:]
    middle = tokens_ref[...].astype(jnp.float32) + (
        own_ref[...].astype(jnp.float32) + other_ref[...].astype(jnp.float32)
    )
    normed, inverse = norm_of(middle)
    gradient = own_grad_ref[...].astype(jnp.float32) + other_grad_ref[...].astype(jnp.float32)
    back = norm_back(gradient, normed, inverse, gain_ref[...])
    gradient = (cot_ref[...].astype(jnp.float32) + back).astype(jnp.bfloat16)
    grad_ref[...] = gradient
    context_grad_ref[...] = contract(gradient, out_w[...], 1, 0).astype(jnp.bfloat16)


def middle_back(tokens, own, other, own_grad, other_grad, cotangent, gain, out_w, start, tile, earlier=()):
    rows, model = own.shape
    width, first = out_w.shape[1], start // tile
    row_block = pl.BlockSpec((tile, model), lambda i: (i, 0))
    late_block = pl.BlockSpec((tile, model), lambda i: (first + i, 0))
    return pl.pallas_call(
        middle_back_kernel,
        grid=(rows // tile,),
        in_specs=[
            late_block, row_block, row_block, row_block, row_block, late_block,
            pl.BlockSpec((1, model), lambda i: (0, 0)),
            pl.BlockSpec((model, width), lambda i: (0, 0), pipeline_mode=pl.Buffered(1)),
        ]
        + [pl.BlockSpec(memory_space=pl.ANY)] * len(earlier),
        out_specs=[late_block, pl.BlockSpec((tile, width), lambda i: (first + i, 0))],
        out_shape=[
            jax.ShapeDtypeStruct(tokens.shape, jnp.bfloat16),
            jax.ShapeDtypeStruct((tokens.shape[0], width), jnp.bfloat16),
        ],
        input_output_aliases={8 + at: at for at in range(len(earlier))},
        compiler_params=pltpu.CompilerParams(vmem_limit_bytes=VMEM_BYTES),
        cost_estimate=pl.CostEstimate(
            flops=2 * rows * model * width, bytes_accessed=2 * (7 * rows * model + model * width), transcendentals=0
        ),
        name="middle_back",
    )(tokens, own, other, own_grad, other_grad, cotangent, gain, out_w, *earlier)


def last_kernel(tokens_ref, own_grad_ref, other_grad_ref, above_ref, gain_ref, grad_ref):
    normed, inverse = norm_of(tokens_ref[...].astype(jnp.float32))
    gradient = own_grad_ref[...].astype(jnp.float32) + other_grad_ref[...].astype(jnp.float32)
    grad_ref[...] = above_ref[...].astype(jnp.float32) + norm_back(gradient, normed, inverse, gain_ref[...])


def last(tokens, own_grad, other_grad, above, gain, start, tile, earlier=()):
    rows, model = own_grad.shape
    first = start // tile
    row_block = pl.BlockSpec((tile, model), lambda i: (i, 0))
    late_block = pl.BlockSpec((tile, model), lambda i: (first + i, 0))

    def body(*refs):
        last_kernel(*refs[:5], refs[-1])

    return pl.pallas_call(
        body,
        grid=(rows // tile,),
        in_specs=[late_block, row_block, row_block, late_block, pl.BlockSpec((1, model), lambda i: (0, 0))]
        + [pl.BlockSpec(memory_space=pl.ANY)] * len(earlier),
        out_specs=late_block,
        out_shape=jax.ShapeDtypeStruct(tokens.shape, jnp.float32),
        input_output_aliases={5 + at: at for at in range(len(earlier))},
        compiler_params=pltpu.CompilerParams(vmem_limit_bytes=VMEM_BYTES),
        cost_estimate=pl.CostEstimate(flops=20 * rows * model, bytes_accessed=12 * rows * model, transcendentals=0),
        name="last",
    )(tokens, own_grad, other_grad, above, gain, *earlier)


def feed_weights_kernel(hidden_ref, cot_ref, acts_ref, out_ref):
    @pl.when(pl.program_id(0) < 2)
    def _():
        out_ref[...] = contract(hidden_ref[...], acts_ref[...], 0, 0).astype(jnp.bfloat16)

    @pl.when(pl.program_id(0) == 2)
    def _():
        out_ref[...] = contract(cot_ref[...], acts_ref[...], 0, 0).astype(jnp.bfloat16)


def feed_weights(hidden, cotangent, acts, tile):
    count, model = hidden.shape
    size = acts.shape[1] // 3
    return pl.pallas_call(
        feed_weights_kernel,
        grid=(3, model // tile),
        in_specs=[
            pl.BlockSpec((count, tile), lambda j, i: (0, i)),
            pl.BlockSpec((count, tile), lambda j, i: (0, i)),
            pl.BlockSpec((count, size), lambda j, i: (0, j)),
        ],
        out_specs=pl.BlockSpec((tile, size), lambda j, i: (i, j)),
        out_shape=jax.ShapeDtypeStruct((model, 3 * size), jnp.bfloat16),
        compiler_params=pltpu.CompilerParams(vmem_limit_bytes=VMEM_BYTES),
        cost_estimate=pl.CostEstimate(
            flops=6 * count * model * size, bytes_accessed=6 * count * size + 4 * count * model + 6 * model * size,
            transcendentals=0,
        ),
        name="feed_weights",
    )(hidden, cotangent, acts)


def positions(segment_ids):
    index_row = jnp.arange(segment_ids.shape[0], dtype=jnp.int32)
    change = jnp.concatenate([jnp.ones((1,), bool), segment_ids[1:] != segment_ids[:-1]])
    marker = jnp.where(change, index_row, jnp.zeros_like(index_row))
    starts = lax.cummax(marker, axis=0)
    return (index_row - starts).astype(jnp.float32)


def rope_tables(places):
    half = HD // 2
    inverse = ROPE_BASE ** (-2.0 * jnp.arange(half, dtype=jnp.float32) / HD)
    angles = places[:, None] * inverse[None, :]
    cosine, sine = jnp.cos(angles), jnp.sin(angles)
    return (
        jnp.concatenate([cosine] * 4, axis=1),
        jnp.concatenate([-sine, sine, -sine, sine], axis=1),
    )


def shifted(count, inner, step):
    return [(a * inner + b, (a + step) % count * inner + b) for a in range(count) for b in range(inner)]


def flipped(count, bit):
    return [(i, i ^ bit) for i in range(count)]


def place_of(count):
    here = lax.axis_index("dp")
    return here // 4, (here // 2) % 2, here % 2, count // 4


def gather_pieces(shard, after=None):
    count = lax.axis_size("dp")
    if count % 4:
        return [lax.all_gather(shard, "dp", axis=0, tiled=True)], jnp.zeros((1,), jnp.int32), shard
    if after is not None:
        shard, _ = lax.optimization_barrier((shard, after))
    outer, pair, core, outers = place_of(count)
    pieces = [(shard, outer, pair)]
    for back in range(1, outers):
        moved = lax.ppermute(shard, "dp", shifted(outers, 4, back))
        pieces.append((moved, (outer - back) % outers, pair))
    for piece, outer_at, _ in list(pieces):
        pieces.append((lax.ppermute(piece, "dp", flipped(count, 2)), outer_at, 1 - pair))
    arrived = [piece for piece, _, _ in pieces[outers:]]
    found, places = [], []
    for piece, outer_at, pair_at in pieces:
        found += [piece, lax.ppermute(piece, "dp", flipped(count, 1))]
        chip = (outer_at * 2 + pair_at) * 2
        places += [chip + core, chip + 1 - core]
    return found, jnp.stack(places).astype(jnp.int32), arrived


def scatter_product(left, rights):
    count = lax.axis_size("dp")
    if count % 4:
        partial = jnp.concatenate([contract(left, right, 0, 0) for right in rights], axis=1).astype(jnp.bfloat16)
        return lax.psum_scatter(partial, "dp", scatter_dimension=0, tiled=True).astype(jnp.float32)
    outer, pair, core, outers = place_of(count)
    kept, sent = parted_weights(left, rights, core.astype(jnp.int32)[None], outers)
    got = lax.ppermute(sent, "dp", flipped(count, 1))
    rows = left.shape[1] // count
    kept, got = (values.reshape(outers, 2, rows, -1) for values in (kept, got))

    def total_at(kept, got, at, axis):
        pick = lambda values: lax.dynamic_index_in_dim(values, at, axis, keepdims=False).astype(jnp.float32)
        return pick(kept) + pick(got)

    sent = total_at(kept, got, 1 - pair, 1).astype(jnp.bfloat16)
    kept = total_at(kept, got, pair, 1).astype(jnp.bfloat16)
    got = lax.ppermute(sent, "dp", flipped(count, 2))
    total = total_at(kept, got, outer, 0)
    moved = []
    for step in range(1, outers):
        sent = total_at(kept, got, (outer + step) % outers, 0).astype(jnp.bfloat16)
        moved.append(lax.ppermute(sent, "dp", shifted(outers, 4, step)))
    return total + sum(values.astype(jnp.float32) for values in moved)


def whole_sum(values, mp_size):
    count = lax.axis_size("dp")
    if count % 4 or mp_size != 2:
        return lax.psum(values, ("dp", "mp"))
    values = values + lax.ppermute(values, "dp", flipped(count, 1))
    values = values + lax.ppermute(values, "dp", flipped(count, 2))
    moved = [lax.ppermute(values, "dp", shifted(count // 4, 4, step)) for step in range(1, count // 4)]
    values = values + sum(moved)
    return values + lax.ppermute(values, "mp", [(0, 1), (1, 0)])


def from_pair(rounded):
    if lax.axis_size("mp") != 2:
        total = lax.psum(rounded, "mp").astype(jnp.float32) - rounded.astype(jnp.float32)
        return total.astype(rounded.dtype)
    return lax.ppermute(rounded, "mp", [(0, 1), (1, 0)])


def layer(tokens, segment_ids, attn_gain, w_qkv, w_out, mlp_gain, w_in, w_ff_out, cotangent):
    count, _ = tokens.shape
    shard_rows, width, hidden_here = w_qkv.shape[0], w_qkv.shape[2], w_in.shape[2]
    spare = -hidden_here % LANES
    size = hidden_here + spare
    half, tile = count // 2, count // 4
    starts = (0, half)

    def padded(values):
        return jnp.pad(values, ((0, 0), (0, spare)))

    gains = jnp.pad(jnp.stack([attn_gain, mlp_gain], axis=1), ((0, 0), (0, LANES - 2)))
    pieces, places, arrived = gather_pieces(jnp.concatenate([w_qkv.reshape(shard_rows, -1), gains], axis=1))
    out_pieces, out_places, _ = gather_pieces(w_out.T, arrived)
    ffn_full = lax.all_gather(
        jnp.concatenate([padded(w_in[:, 0]), padded(w_in[:, 1]), padded(w_ff_out.T)], axis=1),
        "dp",
        axis=0,
        tiled=True,
    )
    tables = rope_tables(positions(segment_ids))
    seg_col, seg_row = segment_ids[:, None], segment_ids[None, :]
    hidden_one, projected, qkv_w, gain_rows = project(tokens, pieces, places, tile)
    gain_one, gain_two = gain_rows[0:1], gain_rows[1:2]
    out_w = assemble(out_pieces, out_places)

    kept, own, other = (), [], []
    for start in starts:
        part, *kept = attend(projected, tables, seg_col, seg_row, start, half, tile, kept)
        own.append(contract(part, out_w, 1, 1).astype(jnp.bfloat16))
        other.append(from_pair(own[-1]))
    context, totals = kept

    kept, outs, grads, other_grads, gain_two_grad = (), [], [], [], 0.0
    for at, start in enumerate(starts):
        *kept, out, grad, gain_grad = feed(tokens, own[at], other[at], cotangent, gain_two, ffn_full, start, tile, kept)
        outs.append(out)
        grads.append(grad)
        other_grads.append(from_pair(grad))
        gain_two_grad = gain_two_grad + gain_grad
    hidden_two, acts = kept
    feed_grads = feed_weights(hidden_two, cotangent, acts, tile)
    ffn_total = lax.psum_scatter(feed_grads, "dp", scatter_dimension=0, tiled=True).astype(jnp.float32)

    kept = ()
    for at, start in enumerate(starts):
        kept = middle_back(
            tokens, own[at], other[at], grads[at], other_grads[at], cotangent, gain_two, out_w, start, tile, kept
        )
    attn_grad_in, context_grad = kept
    outs, _ = lax.optimization_barrier((outs, other_grads[-1]))
    other_outs = []
    for out in outs:
        other_outs.append(from_pair(out))
    out_total = scatter_product(attn_grad_in, [context])

    pairs = width // LANES
    groups = 2 if pairs % 2 == 0 else 1
    taken = pairs // groups
    qkv_grads, qkv_total = [], []
    for at in range(groups):
        found = attend_back(
            projected, tables, seg_col, seg_row, context_grad, context, totals, at * taken, taken, count
        )
        qkv_grads += found
        qkv_total.append(scatter_product(hidden_one, found).reshape(shard_rows, 3, -1))
    one_own, one_other, gain_one_grad = [], [], 0.0
    for start in starts:
        partial, gain_grad = project_back(tokens, qkv_grads, qkv_w, start, half, tile)
        gain_one_grad = gain_one_grad + gain_grad
        one_own.append(partial)
        one_other.append(from_pair(partial))
    gain_total = whole_sum(jnp.concatenate([gain_one_grad, gain_two_grad]), lax.axis_size("mp"))
    gain_total = lax.dynamic_slice_in_dim(gain_total, lax.axis_index("dp") * shard_rows, shard_rows, axis=1)
    input_grad = ()
    for at, start in enumerate(starts):
        input_grad = (
            last(tokens, one_own[at], one_other[at], attn_grad_in, gain_one, start, tile, input_grad),
        )
    output = jnp.concatenate(
        [
            (
                tokens[start : start + half].astype(jnp.float32)
                + own[at].astype(jnp.float32)
                + other[at].astype(jnp.float32)
                + outs[at].astype(jnp.float32)
                + other_outs[at].astype(jnp.float32)
            ).astype(jnp.bfloat16)
            for at, start in enumerate(starts)
        ]
    )
    return (
        output,
        input_grad[0],
        gain_total[0],
        jnp.concatenate(qkv_total, axis=2),
        out_total.T,
        gain_total[1],
        jnp.stack([ffn_total[:, :hidden_here], ffn_total[:, size : size + hidden_here]], axis=1),
        ffn_total[:, 2 * size : 2 * size + hidden_here].T,
    )


def solution(mesh):
    return jax.shard_map(
        layer,
        mesh=mesh,
        in_specs=(
            P("dp", None),
            P("dp"),
            P("dp"),
            P("dp", None, "mp"),
            P("mp", "dp"),
            P("dp"),
            P("dp", None, "mp"),
            P("mp", "dp"),
            P("dp", None),
        ),
        out_specs=(
            P("dp", None),
            P("dp", None),
            P("dp"),
            P("dp", None, "mp"),
            P("mp", "dp"),
            P("dp"),
            P("dp", None, "mp"),
            P("mp", "dp"),
        ),
        check_vma=False,
    )
```

```python
import functools

import jax
import jax.numpy as jnp
from jax import lax
from jax.experimental import pallas as pl
from jax.experimental.pallas import tpu as pltpu
from jax.sharding import PartitionSpec as P


HD = 64
LANES = 128
EPSILON = 1e-05
ROPE_BASE = 160000.0
NEGATIVE = -1e30
VMEM_BYTES = 60 * 1024 * 1024


def contract(left, right, left_axis, right_axis, **kwargs):
    return lax.dot_general(
        left, right, (((left_axis,), (right_axis,)), ((), ())), preferred_element_type=jnp.float32, **kwargs
    )


def lane_of(rows):
    return lax.broadcasted_iota(jnp.int32, (rows, LANES), 1)


def partner(values):
    front = lane_of(values.shape[0]) % HD < HD // 2
    return jnp.where(
        front, pltpu.roll(values, LANES - HD // 2, 1), pltpu.roll(values, HD // 2, 1)
    )


def rotate(values, cosine, signed_sine):
    return values * cosine + partner(values) * signed_sine


def unrotate(gradient, cosine, signed_sine):
    return gradient * cosine - partner(gradient) * signed_sine


def attend_kernel(
    heads, query_ref, key_ref, value_ref, cos_tile, sin_tile, cos_ref, sin_ref, seg_col, seg_row,
    *refs,
):
    context_ref, whole_ref, total_ref, keys, values = refs[-5:]
    score_scale = HD ** (-0.5)

    @pl.when(pl.program_id(0) == 0)
    def _():
        for pair in range(heads // 2):
            cols = slice(pair * LANES, (pair + 1) * LANES)
            keys[:, cols] = rotate(key_ref[:, cols], cos_ref[...], sin_ref[...]).astype(jnp.bfloat16)
        values[...] = value_ref[...].astype(jnp.bfloat16)

    rows = query_ref.shape[0]
    lane = lane_of(rows)
    allowed = seg_col[...] == seg_row[...]
    totals = jnp.zeros((rows, LANES), jnp.float32)
    for pair in range(heads // 2):
        cols = slice(pair * LANES, (pair + 1) * LANES)
        query = rotate(query_ref[:, cols], cos_tile[...], sin_tile[...]) * score_scale
        context = jnp.zeros((rows, LANES), jnp.float32)
        for half in range(2):
            own = lane // HD == half
            scores = contract(jnp.where(own, query, 0.0).astype(jnp.bfloat16), keys[:, cols], 1, 1)
            scores = jnp.where(allowed, scores, NEGATIVE)
            peak = jnp.max(scores, axis=-1, keepdims=True)
            weights = jnp.exp(scores - peak)
            total = jnp.sum(weights, axis=-1, keepdims=True)
            mixed = contract(weights.astype(jnp.bfloat16), values[:, cols], 1, 0)
            context = jnp.where(own, mixed / total, context)
            totals = jnp.where(lane == 2 * pair + half, peak + jnp.log(total), totals)
        context_ref[:, cols] = context.astype(jnp.bfloat16)
        whole_ref[:, cols] = context.astype(jnp.bfloat16)
    total_ref[...] = totals.T[:heads]


def attend(projected, tables, seg_col, seg_row, start, rows, tile, earlier=()):
    count, width = projected.shape[0], projected.shape[1] // 3
    heads = width // HD
    first = start // tile
    fixed = dict(pipeline_mode=pl.Buffered(1))
    return pl.pallas_call(
        functools.partial(attend_kernel, heads),
        grid=(rows // tile,),
        in_specs=[
            pl.BlockSpec((tile, width), lambda i: (first + i, 0)),
            pl.BlockSpec((count, width), lambda i: (0, 1), **fixed),
            pl.BlockSpec((count, width), lambda i: (0, 2), **fixed),
            pl.BlockSpec((tile, LANES), lambda i: (first + i, 0)),
            pl.BlockSpec((tile, LANES), lambda i: (first + i, 0)),
            pl.BlockSpec((count, LANES), lambda i: (0, 0), **fixed),
            pl.BlockSpec((count, LANES), lambda i: (0, 0), **fixed),
            pl.BlockSpec((tile, 1), lambda i: (first + i, 0)),
            pl.BlockSpec((1, count), lambda i: (0, 0), **fixed),
        ]
        + [pl.BlockSpec(memory_space=pl.ANY)] * len(earlier),
        out_specs=[
            pl.BlockSpec((tile, width), lambda i: (i, 0)),
            pl.BlockSpec((tile, width), lambda i: (first + i, 0)),
            pl.BlockSpec((heads, tile), lambda i: (0, first + i)),
        ],
        out_shape=[
            jax.ShapeDtypeStruct((rows, width), jnp.bfloat16),
            jax.ShapeDtypeStruct((count, width), jnp.bfloat16),
            jax.ShapeDtypeStruct((heads, count), jnp.float32),
        ],
        input_output_aliases={9 + at: 1 + at for at in range(len(earlier))},
        scratch_shapes=[pltpu.VMEM((count, width), jnp.bfloat16), pltpu.VMEM((count, width), jnp.bfloat16)],
        compiler_params=pltpu.CompilerParams(vmem_limit_bytes=VMEM_BYTES),
        cost_estimate=pl.CostEstimate(
            flops=8 * rows * count * width,
            bytes_accessed=4 * count * width * 3 + 2 * rows * width,
            transcendentals=rows * count * heads,
        ),
        name="attend",
    )(projected, projected, projected, *tables, *tables, seg_col, seg_row, *earlier)


def attend_back_kernel(
    query_ref, key_ref, value_ref, cos_tile, sin_tile, cos_ref, sin_ref, seg_col, seg_row,
    upstream_ref, context_ref, total_ref, query_out, key_out, value_out, keys, values, key_grad, value_grad, *, first
):
    score_scale = HD ** (-0.5)
    pair, step = first + pl.program_id(0), pl.program_id(1)

    @pl.when(step == 0)
    def _():
        keys[...] = rotate(key_ref[...], cos_ref[...], sin_ref[...]).astype(jnp.bfloat16)
        values[...] = value_ref[...].astype(jnp.bfloat16)
        key_grad[...] = jnp.zeros_like(key_grad)
        value_grad[...] = jnp.zeros_like(value_grad)

    rows = query_ref.shape[0]
    lane = lane_of(rows)
    allowed = seg_col[...] == seg_row[...]
    query = rotate(query_ref[...], cos_tile[...], sin_tile[...]) * score_scale
    upstream = upstream_ref[...].astype(jnp.float32)
    product = upstream * context_ref[...].astype(jnp.float32)
    query_grad = jnp.zeros((rows, LANES), jnp.float32)
    for half in range(2):
        own = lane // HD == half
        own_query = jnp.where(own, query, 0.0).astype(jnp.bfloat16)
        own_upstream = jnp.where(own, upstream, 0.0).astype(jnp.bfloat16)
        picks = (lane_of(8) // HD == half).astype(jnp.float32)
        delta = contract(picks, product, 1, 1, precision=lax.Precision.HIGHEST)[0:1]
        total = total_ref[pl.ds(2 * pair + half, 1), :]
        scores = contract(keys[...], own_query, 1, 1)
        probs = jnp.where(allowed, jnp.exp(scores - total), 0.0)
        prob_grad = contract(values[...], own_upstream, 1, 1)
        score_grad = (probs * (prob_grad - delta)).astype(jnp.bfloat16)
        value_grad[...] += contract(probs.astype(jnp.bfloat16), own_upstream, 1, 0)
        key_grad[...] += contract(score_grad, own_query, 1, 0)
        spread = contract(score_grad, keys[...], 0, 0)
        query_grad = jnp.where(own, spread, query_grad)
    query_out[...] = unrotate(query_grad * score_scale, cos_tile[...], sin_tile[...]).astype(jnp.bfloat16)

    @pl.when(step == pl.num_programs(1) - 1)
    def _():
        key_out[...] = unrotate(key_grad[...], cos_ref[...], sin_ref[...]).astype(jnp.bfloat16)
        value_out[...] = value_grad[...].astype(jnp.bfloat16)


def attend_back(projected, tables, seg_col, seg_row, upstream, context, totals, first, taken, tile):
    count, width = projected.shape[0], projected.shape[1] // 3
    heads, pairs = width // HD, width // LANES
    fixed = dict(pipeline_mode=pl.Buffered(1))
    row_block = pl.BlockSpec((tile, LANES), lambda p, i: (i, first + p))
    whole_block = pl.BlockSpec((count, LANES), lambda p, i: (0, p))
    return pl.pallas_call(
        functools.partial(attend_back_kernel, first=first),
        grid=(taken, count // tile),
        in_specs=[
            row_block,
            pl.BlockSpec((count, LANES), lambda p, i: (0, pairs + first + p)),
            pl.BlockSpec((count, LANES), lambda p, i: (0, 2 * pairs + first + p)),
            pl.BlockSpec((tile, LANES), lambda p, i: (i, 0)),
            pl.BlockSpec((tile, LANES), lambda p, i: (i, 0)),
            pl.BlockSpec((count, LANES), lambda p, i: (0, 0), **fixed),
            pl.BlockSpec((count, LANES), lambda p, i: (0, 0), **fixed),
            pl.BlockSpec((count, 1), lambda p, i: (0, 0), **fixed),
            pl.BlockSpec((1, tile), lambda p, i: (0, i)),
            row_block,
            row_block,
            pl.BlockSpec((heads, tile), lambda p, i: (0, i)),
        ],
        out_specs=[pl.BlockSpec((tile, LANES), lambda p, i: (i, p)), whole_block, whole_block],
        out_shape=[jax.ShapeDtypeStruct((count, taken * LANES), jnp.bfloat16)] * 3,
        scratch_shapes=[
            pltpu.VMEM((count, LANES), jnp.bfloat16),
            pltpu.VMEM((count, LANES), jnp.bfloat16),
            pltpu.VMEM((count, LANES), jnp.float32),
            pltpu.VMEM((count, LANES), jnp.float32),
        ],
        compiler_params=pltpu.CompilerParams(vmem_limit_bytes=VMEM_BYTES),
        cost_estimate=pl.CostEstimate(
            flops=20 * count * count * taken * LANES,
            bytes_accessed=22 * count * taken * LANES,
            transcendentals=2 * count * count * taken,
        ),
        name="attend_back",
    )(projected, projected, projected, *tables, *tables, seg_col, seg_row, upstream, context, totals)


def feed_kernel(
    tokens_ref, own_ref, other_ref, cot_ref, gain_ref, gate_w, up_w, down_w,
    *refs,
):
    hidden_ref, acts_ref, out_ref, grad_ref, gain_grad_ref = refs[-5:]
    middle = tokens_ref[...].astype(jnp.float32) + (
        own_ref[...].astype(jnp.float32) + other_ref[...].astype(jnp.float32)
    )
    center = middle - jnp.mean(middle, axis=-1, keepdims=True)
    normed = center * lax.rsqrt(jnp.mean(center * center, axis=-1, keepdims=True) + EPSILON)
    hidden = (normed * gain_ref[...]).astype(jnp.bfloat16)
    hidden_ref[...] = hidden
    gate = contract(hidden, gate_w[...], 1, 0)
    upward = contract(hidden, up_w[...], 1, 0)
    mixed_grad = contract(cot_ref[...], down_w[...], 1, 0)
    share = 0.5 * (1.0 + lax.erf(gate * 0.7071067811865476))
    active = gate * share
    slope = share + gate * jnp.exp(-0.5 * gate * gate) * 0.3989422804014327
    size = gate.shape[1]
    gate_grad = (mixed_grad * upward * slope).astype(jnp.bfloat16)
    up_grad = (mixed_grad * active).astype(jnp.bfloat16)
    mixed = (active * upward).astype(jnp.bfloat16)
    acts_ref[:, :size] = gate_grad
    acts_ref[:, size : 2 * size] = up_grad
    acts_ref[:, 2 * size :] = mixed
    out_ref[...] = contract(mixed, down_w[...], 1, 1).astype(jnp.bfloat16)
    partial = contract(gate_grad, gate_w[...], 1, 1) + contract(up_grad, up_w[...], 1, 1)
    grad_ref[...] = partial.astype(jnp.bfloat16)

    @pl.when(pl.program_id(0) == 0)
    def _():
        gain_grad_ref[...] = jnp.zeros_like(gain_grad_ref)

    gain_grad_ref[...] += jnp.sum(partial * normed, axis=0, keepdims=True)


def feed(tokens, own, other, cotangent, gain, ffn_full, start, tile, earlier=()):
    rows, model = own.shape
    size = ffn_full.shape[1] // 3
    first = start // tile
    fixed = dict(pipeline_mode=pl.Buffered(1))
    row_block = pl.BlockSpec((tile, model), lambda i: (i, 0))
    late_block = pl.BlockSpec((tile, model), lambda i: (first + i, 0))
    return pl.pallas_call(
        feed_kernel,
        grid=(rows // tile,),
        in_specs=[
            late_block, row_block, row_block, late_block,
            pl.BlockSpec((1, model), lambda i: (0, 0), **fixed),
            pl.BlockSpec((model, size), lambda i: (0, 0), **fixed),
            pl.BlockSpec((model, size), lambda i: (0, 1), **fixed),
            pl.BlockSpec((model, size), lambda i: (0, 2), **fixed),
        ]
        + [pl.BlockSpec(memory_space=pl.ANY)] * len(earlier),
        out_specs=[
            late_block,
            pl.BlockSpec((tile, 3 * size), lambda i: (first + i, 0)),
            row_block, row_block,
            pl.BlockSpec((1, model), lambda i: (0, 0)),
        ],
        out_shape=[
            jax.ShapeDtypeStruct(tokens.shape, jnp.bfloat16),
            jax.ShapeDtypeStruct((tokens.shape[0], 3 * size), jnp.bfloat16),
            jax.ShapeDtypeStruct((rows, model), jnp.bfloat16),
            jax.ShapeDtypeStruct((rows, model), jnp.bfloat16),
            jax.ShapeDtypeStruct((1, model), jnp.float32),
        ],
        input_output_aliases={8 + at: at for at in range(len(earlier))},
        compiler_params=pltpu.CompilerParams(vmem_limit_bytes=VMEM_BYTES),
        cost_estimate=pl.CostEstimate(
            flops=12 * rows * model * size,
            bytes_accessed=2 * (3 * model * size + 7 * rows * model + 3 * rows * size),
            transcendentals=2 * rows * size,
        ),
        name="feed",
    )(tokens, own, other, cotangent, gain, ffn_full, ffn_full, ffn_full, *earlier)


def norm_of(values):
    center = values - jnp.mean(values, axis=-1, keepdims=True)
    inverse = lax.rsqrt(jnp.mean(center * center, axis=-1, keepdims=True) + EPSILON)
    return center * inverse, inverse


def norm_back(gradient, normed, inverse, gain):
    scaled = gradient * gain
    return inverse * (
        scaled
        - jnp.mean(scaled, axis=-1, keepdims=True)
        - normed * jnp.mean(scaled * normed, axis=-1, keepdims=True)
    )


def project_kernel(count, places_ref, tokens_ref, *refs):
    pieces = refs[:count]
    hidden_ref, projected_ref, weight_ref, gain_ref, columns = refs[count:]
    rows, width = pieces[0].shape[0], weight_ref.shape[1]

    @pl.when(pl.program_id(0) == 0)
    def _():
        for index, piece in enumerate(pieces):
            at = pl.ds(pl.multiple_of(places_ref[index] * rows, rows), rows)
            weight_ref[at, :] = piece[:, :width]
            columns[at, :] = piece[:, width:].astype(jnp.float32)
        gain_ref[...] = columns[...].T[: gain_ref.shape[0]]

    normed, _ = norm_of(tokens_ref[...].astype(jnp.float32))
    hidden = (normed * gain_ref[0:1]).astype(jnp.bfloat16)
    hidden_ref[...] = hidden
    projected_ref[...] = contract(hidden, weight_ref[...], 1, 0)


def project(tokens, pieces, places, tile):
    (count, model), width = tokens.shape, pieces[0].shape[1] - LANES
    fixed = dict(pipeline_mode=pl.Buffered(1))
    return pl.pallas_call(
        functools.partial(project_kernel, len(pieces)),
        grid=(count // tile,),
        in_specs=[pl.BlockSpec(memory_space=pltpu.SMEM), pl.BlockSpec((tile, model), lambda i: (i, 0))]
        + [pl.BlockSpec(piece.shape, lambda i: (0, 0), **fixed) for piece in pieces],
        out_specs=[
            pl.BlockSpec((tile, model), lambda i: (i, 0)),
            pl.BlockSpec((tile, width), lambda i: (i, 0)),
            pl.BlockSpec((model, width), lambda i: (0, 0)),
            pl.BlockSpec((8, model), lambda i: (0, 0)),
        ],
        out_shape=[
            jax.ShapeDtypeStruct((count, model), jnp.bfloat16),
            jax.ShapeDtypeStruct((count, width), jnp.float32),
            jax.ShapeDtypeStruct((model, width), jnp.bfloat16),
            jax.ShapeDtypeStruct((8, model), jnp.float32),
        ],
        scratch_shapes=[pltpu.VMEM((model, LANES), jnp.float32)],
        compiler_params=pltpu.CompilerParams(vmem_limit_bytes=VMEM_BYTES),
        cost_estimate=pl.CostEstimate(
            flops=2 * count * model * width,
            bytes_accessed=4 * count * model + 4 * count * width + 4 * model * width,
            transcendentals=0,
        ),
        name="project",
    )(places, tokens, *pieces)


def project_out_kernel(places_ref, context_ref, *refs):
    *pieces, partial_ref, weight_ref = refs
    rows = pieces[0].shape[0]
    for index, piece in enumerate(pieces):
        weight_ref[pl.ds(pl.multiple_of(places_ref[index] * rows, rows), rows), :] = piece[...]
    partial_ref[...] = contract(context_ref[...], weight_ref[...], 1, 1).astype(jnp.bfloat16)


def project_out(context, pieces, places):
    rows, width = pieces[0].shape
    model = len(pieces) * rows
    whole = pl.BlockSpec(memory_space=pltpu.VMEM)
    return pl.pallas_call(
        project_out_kernel,
        in_specs=[pl.BlockSpec(memory_space=pltpu.SMEM)] + [whole] * (1 + len(pieces)),
        out_specs=[whole, whole],
        out_shape=[
            jax.ShapeDtypeStruct((context.shape[0], model), jnp.bfloat16),
            jax.ShapeDtypeStruct((model, width), jnp.bfloat16),
        ],
        compiler_params=pltpu.CompilerParams(vmem_limit_bytes=VMEM_BYTES),
        cost_estimate=pl.CostEstimate(
            flops=2 * context.shape[0] * model * width,
            bytes_accessed=4 * model * width + 2 * context.shape[0] * (model + width),
            transcendentals=0,
        ),
        name="project_out",
    )(places, context, *pieces)


def project_back_kernel(groups, tokens_ref, weight_ref, *refs):
    grads, (out_ref, gain_grad_ref) = refs[: 3 * groups], refs[3 * groups :]
    size = grads[0].shape[1]
    partial = 0.0
    for at, ref in enumerate(grads):
        begin = (at % 3 * groups + at // 3) * size
        partial = partial + contract(ref[...], weight_ref[:, begin : begin + size], 1, 1)
    out_ref[...] = partial.astype(jnp.bfloat16)
    normed, _ = norm_of(tokens_ref[...].astype(jnp.float32))

    @pl.when(pl.program_id(0) == 0)
    def _():
        gain_grad_ref[...] = jnp.zeros_like(gain_grad_ref)

    gain_grad_ref[...] += jnp.sum(partial * normed, axis=0, keepdims=True)


def project_back(tokens, grads, weight, start, rows, tile):
    model, first = tokens.shape[1], start // tile
    late = lambda i: (first + i, 0)
    return pl.pallas_call(
        functools.partial(project_back_kernel, len(grads) // 3),
        grid=(rows // tile,),
        in_specs=[
            pl.BlockSpec((tile, model), late),
            pl.BlockSpec(weight.shape, lambda i: (0, 0), pipeline_mode=pl.Buffered(1)),
        ]
        + [pl.BlockSpec((tile, grad.shape[1]), late) for grad in grads],
        out_specs=[pl.BlockSpec((tile, model), lambda i: (i, 0)), pl.BlockSpec((1, model), lambda i: (0, 0))],
        out_shape=[jax.ShapeDtypeStruct((rows, model), jnp.bfloat16), jax.ShapeDtypeStruct((1, model), jnp.float32)],
        compiler_params=pltpu.CompilerParams(vmem_limit_bytes=VMEM_BYTES),
        cost_estimate=pl.CostEstimate(
            flops=2 * rows * model * weight.shape[1],
            bytes_accessed=4 * rows * model + 2 * (rows + model) * weight.shape[1],
            transcendentals=0,
        ),
        name="project_back",
    )(tokens, weight, *grads)


def parted_weights_kernel(core_ref, hidden_ref, gradient_ref, *refs):
    rights, outs = refs[:4], refs[4:]
    first_core = core_ref[0] == 0
    rows = hidden_ref.shape[1] // 4
    width = rights[0].shape[1]
    for index, right in enumerate(rights):
        left_ref = gradient_ref if index == 3 else hidden_ref
        product = contract(left_ref[...], right[...], 0, 0).astype(jnp.bfloat16)
        kept_ref, sent_ref = outs[index // 2 * 2 : index // 2 * 2 + 2]
        cols = slice(index % 2 * width, (index % 2 + 1) * width)
        for pair in range(2):
            even = product[2 * pair * rows : (2 * pair + 1) * rows]
            odd = product[(2 * pair + 1) * rows : (2 * pair + 2) * rows]
            at = slice(pair * rows, (pair + 1) * rows)
            kept_ref[at, cols] = jnp.where(first_core, even, odd)
            sent_ref[at, cols] = jnp.where(first_core, odd, even)


def parted_weights(hidden, gradient, rights, core, outers):
    count, model = hidden.shape
    width = rights[0].shape[1]
    tile = model // outers
    half_block = pl.BlockSpec((tile // 2, 2 * width), lambda i: (i, 0))
    left_block = pl.BlockSpec((count, tile), lambda i: (0, i))
    return pl.pallas_call(
        parted_weights_kernel,
        grid=(outers,),
        in_specs=[pl.BlockSpec(memory_space=pltpu.SMEM), left_block, left_block]
        + [pl.BlockSpec(right.shape, lambda i: (0, 0), pipeline_mode=pl.Buffered(1)) for right in rights],
        out_specs=[half_block] * 4,
        out_shape=[jax.ShapeDtypeStruct((model // 2, 2 * width), jnp.bfloat16)] * 4,
        compiler_params=pltpu.CompilerParams(vmem_limit_bytes=VMEM_BYTES),
        cost_estimate=pl.CostEstimate(
            flops=8 * count * model * width, bytes_accessed=8 * (count + model) * width + 4 * count * model,
            transcendentals=0,
        ),
        name="parted_weights",
    )(core, hidden, gradient, *rights)


def middle_back_kernel(
    tokens_ref, own_ref, other_ref, own_grad_ref, other_grad_ref, cot_ref, gain_ref, out_w, *refs
):
    grad_ref, context_grad_ref = refs[-2:]
    middle = tokens_ref[...].astype(jnp.float32) + (
        own_ref[...].astype(jnp.float32) + other_ref[...].astype(jnp.float32)
    )
    normed, inverse = norm_of(middle)
    gradient = own_grad_ref[...].astype(jnp.float32) + other_grad_ref[...].astype(jnp.float32)
    back = norm_back(gradient, normed, inverse, gain_ref[...])
    gradient = (cot_ref[...].astype(jnp.float32) + back).astype(jnp.bfloat16)
    grad_ref[...] = gradient
    context_grad_ref[...] = contract(gradient, out_w[...], 1, 0).astype(jnp.bfloat16)


def middle_back(tokens, own, other, own_grad, other_grad, cotangent, gain, out_w, start, tile, earlier=()):
    rows, model = own.shape
    width, first = out_w.shape[1], start // tile
    row_block = pl.BlockSpec((tile, model), lambda i: (i, 0))
    late_block = pl.BlockSpec((tile, model), lambda i: (first + i, 0))
    return pl.pallas_call(
        middle_back_kernel,
        grid=(rows // tile,),
        in_specs=[
            late_block, row_block, row_block, row_block, row_block, late_block,
            pl.BlockSpec((1, model), lambda i: (0, 0)),
            pl.BlockSpec((model, width), lambda i: (0, 0), pipeline_mode=pl.Buffered(1)),
        ]
        + [pl.BlockSpec(memory_space=pl.ANY)] * len(earlier),
        out_specs=[late_block, pl.BlockSpec((tile, width), lambda i: (first + i, 0))],
        out_shape=[
            jax.ShapeDtypeStruct(tokens.shape, jnp.bfloat16),
            jax.ShapeDtypeStruct((tokens.shape[0], width), jnp.bfloat16),
        ],
        input_output_aliases={8 + at: at for at in range(len(earlier))},
        compiler_params=pltpu.CompilerParams(vmem_limit_bytes=VMEM_BYTES),
        cost_estimate=pl.CostEstimate(
            flops=2 * rows * model * width, bytes_accessed=2 * (7 * rows * model + model * width), transcendentals=0
        ),
        name="middle_back",
    )(tokens, own, other, own_grad, other_grad, cotangent, gain, out_w, *earlier)


def last_kernel(tokens_ref, own_grad_ref, other_grad_ref, above_ref, gain_ref, grad_ref):
    normed, inverse = norm_of(tokens_ref[...].astype(jnp.float32))
    gradient = own_grad_ref[...].astype(jnp.float32) + other_grad_ref[...].astype(jnp.float32)
    grad_ref[...] = above_ref[...].astype(jnp.float32) + norm_back(gradient, normed, inverse, gain_ref[...])


def last(tokens, own_grad, other_grad, above, gain, start, tile, earlier=()):
    rows, model = own_grad.shape
    first = start // tile
    row_block = pl.BlockSpec((tile, model), lambda i: (i, 0))
    late_block = pl.BlockSpec((tile, model), lambda i: (first + i, 0))

    def body(*refs):
        last_kernel(*refs[:5], refs[-1])

    return pl.pallas_call(
        body,
        grid=(rows // tile,),
        in_specs=[late_block, row_block, row_block, late_block, pl.BlockSpec((1, model), lambda i: (0, 0))]
        + [pl.BlockSpec(memory_space=pl.ANY)] * len(earlier),
        out_specs=late_block,
        out_shape=jax.ShapeDtypeStruct(tokens.shape, jnp.float32),
        input_output_aliases={5 + at: at for at in range(len(earlier))},
        compiler_params=pltpu.CompilerParams(vmem_limit_bytes=VMEM_BYTES),
        cost_estimate=pl.CostEstimate(flops=20 * rows * model, bytes_accessed=12 * rows * model, transcendentals=0),
        name="last",
    )(tokens, own_grad, other_grad, above, gain, *earlier)


def feed_weights_kernel(hidden_ref, cot_ref, acts_ref, out_ref):
    @pl.when(pl.program_id(0) < 2)
    def _():
        out_ref[...] = contract(hidden_ref[...], acts_ref[...], 0, 0).astype(jnp.bfloat16)

    @pl.when(pl.program_id(0) == 2)
    def _():
        out_ref[...] = contract(cot_ref[...], acts_ref[...], 0, 0).astype(jnp.bfloat16)


def feed_weights(hidden, cotangent, acts, tile):
    count, model = hidden.shape
    size = acts.shape[1] // 3
    return pl.pallas_call(
        feed_weights_kernel,
        grid=(3, model // tile),
        in_specs=[
            pl.BlockSpec((count, tile), lambda j, i: (0, i)),
            pl.BlockSpec((count, tile), lambda j, i: (0, i)),
            pl.BlockSpec((count, size), lambda j, i: (0, j)),
        ],
        out_specs=pl.BlockSpec((tile, size), lambda j, i: (i, j)),
        out_shape=jax.ShapeDtypeStruct((model, 3 * size), jnp.bfloat16),
        compiler_params=pltpu.CompilerParams(vmem_limit_bytes=VMEM_BYTES),
        cost_estimate=pl.CostEstimate(
            flops=6 * count * model * size, bytes_accessed=6 * count * size + 4 * count * model + 6 * model * size,
            transcendentals=0,
        ),
        name="feed_weights",
    )(hidden, cotangent, acts)


def positions(segment_ids):
    index_row = jnp.arange(segment_ids.shape[0], dtype=jnp.int32)
    change = jnp.concatenate([jnp.ones((1,), bool), segment_ids[1:] != segment_ids[:-1]])
    marker = jnp.where(change, index_row, jnp.zeros_like(index_row))
    starts = lax.cummax(marker, axis=0)
    return (index_row - starts).astype(jnp.float32)


def rope_tables(places):
    half = HD // 2
    inverse = ROPE_BASE ** (-2.0 * jnp.arange(half, dtype=jnp.float32) / HD)
    angles = places[:, None] * inverse[None, :]
    cosine, sine = jnp.cos(angles), jnp.sin(angles)
    return (
        jnp.concatenate([cosine] * 4, axis=1),
        jnp.concatenate([-sine, sine, -sine, sine], axis=1),
    )


def shifted(count, inner, step):
    return [(a * inner + b, (a + step) % count * inner + b) for a in range(count) for b in range(inner)]


def flipped(count, bit):
    return [(i, i ^ bit) for i in range(count)]


def place_of(count):
    here = lax.axis_index("dp")
    return here // 4, (here // 2) % 2, here % 2, count // 4


def gather_pieces(shard, after=None, ahead=None):
    count = lax.axis_size("dp")
    if count % 4:
        return [lax.all_gather(shard, "dp", axis=0, tiled=True)], jnp.zeros((1,), jnp.int32), shard, ahead
    if after is not None:
        shard, _ = lax.optimization_barrier((shard, after))
    outer, pair, core, outers = place_of(count)
    pieces = [(shard, outer, pair)]
    for back in range(1, outers):
        moved = lax.ppermute(shard, "dp", shifted(outers, 4, back))
        pieces.append((moved, (outer - back) % outers, pair))
    arrived = [piece for piece, _, _ in pieces[1:]]
    for at, (piece, outer_at, _) in enumerate(list(pieces)):
        if at == 2 and ahead is not None:
            piece, ahead = lax.optimization_barrier((piece, ahead))
        pieces.append((lax.ppermute(piece, "dp", flipped(count, 2)), outer_at, 1 - pair))
    found, places = [], []
    for piece, outer_at, pair_at in pieces:
        found += [piece, lax.ppermute(piece, "dp", flipped(count, 1))]
        chip = (outer_at * 2 + pair_at) * 2
        places += [chip + core, chip + 1 - core]
    return found, jnp.stack(places).astype(jnp.int32), arrived, ahead


def scatter_rows(kept, sent):
    count = lax.axis_size("dp")
    outer, pair, _, outers = place_of(count)
    got = lax.ppermute(sent, "dp", flipped(count, 1))
    rows = 2 * kept.shape[0] // count
    kept, got = (values.reshape(outers, 2, rows, -1) for values in (kept, got))

    def total_at(kept, got, at, axis):
        pick = lambda values: lax.dynamic_index_in_dim(values, at, axis, keepdims=False).astype(jnp.float32)
        return pick(kept) + pick(got)

    sent = total_at(kept, got, 1 - pair, 1).astype(jnp.bfloat16)
    kept = total_at(kept, got, pair, 1).astype(jnp.bfloat16)
    got = lax.ppermute(sent, "dp", flipped(count, 2))
    total = total_at(kept, got, outer, 0)
    moved = []
    for step in range(1, outers):
        sent = total_at(kept, got, (outer + step) % outers, 0).astype(jnp.bfloat16)
        moved.append(lax.ppermute(sent, "dp", shifted(outers, 4, step)))
    return total + sum(values.astype(jnp.float32) for values in moved)


def scatter_weights(hidden, gradient, rights):
    count, width = lax.axis_size("dp"), rights[0].shape[1]
    if count % 4:
        lefts = (hidden, hidden, hidden, gradient)
        partial = [contract(left, right, 0, 0) for left, right in zip(lefts, rights)]
        partial = jnp.concatenate(partial, axis=1).astype(jnp.bfloat16)
        total = lax.psum_scatter(partial, "dp", scatter_dimension=0, tiled=True).astype(jnp.float32)
        return [total[:, at * width : (at + 1) * width] for at in range(4)]
    _, _, core, outers = place_of(count)
    halves = parted_weights(hidden, gradient, rights, core.astype(jnp.int32)[None], outers)
    totals = [scatter_rows(*halves[:2]), scatter_rows(*halves[2:])]
    return [total[:, at * width : (at + 1) * width] for total in totals for at in range(2)]


def whole_sum(values, mp_size):
    count = lax.axis_size("dp")
    if count % 4 or mp_size != 2:
        return lax.psum(values, ("dp", "mp"))
    values = values + lax.ppermute(values, "mp", [(0, 1), (1, 0)])
    values = values + lax.ppermute(values, "dp", flipped(count, 1))
    values = values + lax.ppermute(values, "dp", flipped(count, 2))
    moved = [lax.ppermute(values, "dp", shifted(count // 4, 4, step)) for step in range(1, count // 4)]
    return values + sum(moved)


def from_pair(rounded):
    if lax.axis_size("mp") != 2:
        total = lax.psum(rounded, "mp").astype(jnp.float32) - rounded.astype(jnp.float32)
        return total.astype(rounded.dtype)
    return lax.ppermute(rounded, "mp", [(0, 1), (1, 0)])


def layer(tokens, segment_ids, attn_gain, w_qkv, w_out, mlp_gain, w_in, w_ff_out, cotangent):
    count, _ = tokens.shape
    shard_rows, width, hidden_here = w_qkv.shape[0], w_qkv.shape[2], w_in.shape[2]
    spare = -hidden_here % LANES
    size = hidden_here + spare
    tile = count // 4
    chunks = ((0, tile), (tile, tile), (2 * tile, 2 * tile))
    late_chunks = ((0, tile), (tile, 2 * tile), (3 * tile, tile))

    def padded(values):
        return jnp.pad(values, ((0, 0), (0, spare)))

    gains = jnp.pad(jnp.stack([attn_gain, mlp_gain], axis=1), ((0, 0), (0, LANES - 2)))
    tables = rope_tables(positions(segment_ids))
    first_shard = jnp.concatenate([w_qkv.reshape(shard_rows, -1), gains], axis=1)
    pieces, places, arrived, tables = gather_pieces(first_shard, ahead=tables)
    out_pieces, out_places, *_ = gather_pieces(w_out.T, after=arrived)
    ffn_shard = jnp.concatenate([padded(w_in[:, 0]), padded(w_in[:, 1]), padded(w_ff_out.T)], axis=1)
    ffn_full = lax.all_gather(ffn_shard, "dp", axis=0, tiled=True)
    seg_col, seg_row = segment_ids[:, None], segment_ids[None, :]
    hidden_one, projected, qkv_w, gain_rows = project(tokens, pieces, places, tile)
    gain_one, gain_two = gain_rows[0:1], gain_rows[1:2]

    kept, own, other, out_w = (), [], [], None
    for start, rows in chunks:
        part, *kept = attend(projected, tables, seg_col, seg_row, start, rows, tile, kept)
        if out_w is None:
            partial, out_w = project_out(part, out_pieces, out_places)
        else:
            partial = contract(part, out_w, 1, 1).astype(jnp.bfloat16)
        own.append(partial)
        other.append(from_pair(partial))
    context, totals = kept

    kept, outs, grads, other_grads, gain_two_grad = (), [], [], [], 0.0
    for at, (start, rows) in enumerate(chunks):
        *kept, out, grad, gain_grad = feed(tokens, own[at], other[at], cotangent, gain_two, ffn_full, start, tile, kept)
        outs.append(out)
        grads.append(grad)
        other_grads.append(from_pair(grad))
        gain_two_grad = gain_two_grad + gain_grad
    hidden_two, acts = kept
    feed_grads = feed_weights(hidden_two, cotangent, acts, tile)
    ffn_total = lax.psum_scatter(feed_grads, "dp", scatter_dimension=0, tiled=True).astype(jnp.float32)

    kept = ()
    for at, (start, rows) in enumerate(chunks):
        kept = middle_back(
            tokens, own[at], other[at], grads[at], other_grads[at], cotangent, gain_two, out_w, start, tile, kept
        )
    attn_grad_in, context_grad = kept
    outs, _ = lax.optimization_barrier((outs, other_grads[-1]))
    other_outs = []
    for out in outs:
        other_outs.append(from_pair(out))

    qkv_grads = attend_back(
        projected, tables, seg_col, seg_row, context_grad, context, totals, 0, width // LANES, count
    )
    query_total, key_total, value_total, out_total = scatter_weights(hidden_one, attn_grad_in, [*qkv_grads, context])
    one_own, one_other, gain_one_grad = [], [], 0.0
    for start, rows in late_chunks:
        partial, gain_grad = project_back(tokens, qkv_grads, qkv_w, start, rows, tile)
        gain_one_grad = gain_one_grad + gain_grad
        one_own.append(partial)
        one_other.append(from_pair(partial))
    gain_total = whole_sum(jnp.concatenate([gain_one_grad, gain_two_grad]), lax.axis_size("mp"))
    gain_total = lax.dynamic_slice_in_dim(gain_total, lax.axis_index("dp") * shard_rows, shard_rows, axis=1)
    input_grad = ()
    for at, (start, _) in enumerate(late_chunks):
        input_grad = (
            last(tokens, one_own[at], one_other[at], attn_grad_in, gain_one, start, tile, input_grad),
        )
    output = jnp.concatenate(
        [
            (
                tokens[start : start + rows].astype(jnp.float32)
                + own[at].astype(jnp.float32)
                + other[at].astype(jnp.float32)
                + outs[at].astype(jnp.float32)
                + other_outs[at].astype(jnp.float32)
            ).astype(jnp.bfloat16)
            for at, (start, rows) in enumerate(chunks)
        ]
    )
    return (
        output,
        input_grad[0],
        gain_total[0],
        jnp.stack([query_total, key_total, value_total], axis=1),
        out_total.T,
        gain_total[1],
        jnp.stack([ffn_total[:, :hidden_here], ffn_total[:, size : size + hidden_here]], axis=1),
        ffn_total[:, 2 * size : 2 * size + hidden_here].T,
    )


def solution(mesh):
    return jax.shard_map(
        layer,
        mesh=mesh,
        in_specs=(
            P("dp", None),
            P("dp"),
            P("dp"),
            P("dp", None, "mp"),
            P("mp", "dp"),
            P("dp"),
            P("dp", None, "mp"),
            P("mp", "dp"),
            P("dp", None),
        ),
        out_specs=(
            P("dp", None),
            P("dp", None),
            P("dp"),
            P("dp", None, "mp"),
            P("mp", "dp"),
            P("dp"),
            P("dp", None, "mp"),
            P("mp", "dp"),
        ),
        check_vma=False,
    )
```

```python
import functools

import jax
import jax.numpy as jnp
from jax import lax
from jax.experimental import pallas as pl
from jax.experimental.pallas import tpu as pltpu
from jax.sharding import PartitionSpec as P


HD = 64
LANES = 128
EPSILON = 1e-05
ROPE_BASE = 160000.0
NEGATIVE = -1e30
VMEM_BYTES = 60 * 1024 * 1024


def contract(left, right, left_axis, right_axis, **kwargs):
    return lax.dot_general(
        left, right, (((left_axis,), (right_axis,)), ((), ())), preferred_element_type=jnp.float32, **kwargs
    )


def lane_of(rows):
    return lax.broadcasted_iota(jnp.int32, (rows, LANES), 1)


def partner(values):
    front = lane_of(values.shape[0]) % HD < HD // 2
    return jnp.where(
        front, pltpu.roll(values, LANES - HD // 2, 1), pltpu.roll(values, HD // 2, 1)
    )


def rotate(values, cosine, signed_sine):
    return values * cosine + partner(values) * signed_sine


def unrotate(gradient, cosine, signed_sine):
    return gradient * cosine - partner(gradient) * signed_sine


def attend_kernel(
    heads, query_ref, key_ref, value_ref, cos_tile, sin_tile, cos_ref, sin_ref, seg_col, seg_row,
    *refs,
):
    context_ref, whole_ref, total_ref, keys, values = refs[-5:]
    score_scale = HD ** (-0.5)

    @pl.when(pl.program_id(0) == 0)
    def _():
        for pair in range(heads // 2):
            cols = slice(pair * LANES, (pair + 1) * LANES)
            keys[:, cols] = rotate(key_ref[:, cols], cos_ref[...], sin_ref[...]).astype(jnp.bfloat16)
        values[...] = value_ref[...].astype(jnp.bfloat16)

    rows = query_ref.shape[0]
    lane = lane_of(rows)
    allowed = seg_col[...] == seg_row[...]
    totals = jnp.zeros((rows, LANES), jnp.float32)
    for pair in range(heads // 2):
        cols = slice(pair * LANES, (pair + 1) * LANES)
        query = rotate(query_ref[:, cols], cos_tile[...], sin_tile[...]) * score_scale
        context = jnp.zeros((rows, LANES), jnp.float32)
        for half in range(2):
            own = lane // HD == half
            scores = contract(jnp.where(own, query, 0.0).astype(jnp.bfloat16), keys[:, cols], 1, 1)
            scores = jnp.where(allowed, scores, NEGATIVE)
            peak = jnp.max(scores, axis=-1, keepdims=True)
            weights = jnp.exp(scores - peak)
            total = jnp.sum(weights, axis=-1, keepdims=True)
            mixed = contract(weights.astype(jnp.bfloat16), values[:, cols], 1, 0)
            context = jnp.where(own, mixed / total, context)
            totals = jnp.where(lane == 2 * pair + half, peak + jnp.log(total), totals)
        context_ref[:, cols] = context.astype(jnp.bfloat16)
        whole_ref[:, cols] = context.astype(jnp.bfloat16)
    total_ref[...] = totals.T[:heads]


def attend(projected, tables, seg_col, seg_row, start, rows, tile, earlier=()):
    count, width = projected.shape[0], projected.shape[1] // 3
    heads = width // HD
    first = start // tile
    fixed = dict(pipeline_mode=pl.Buffered(1))
    return pl.pallas_call(
        functools.partial(attend_kernel, heads),
        grid=(rows // tile,),
        in_specs=[
            pl.BlockSpec((tile, width), lambda i: (first + i, 0)),
            pl.BlockSpec((count, width), lambda i: (0, 1), **fixed),
            pl.BlockSpec((count, width), lambda i: (0, 2), **fixed),
            pl.BlockSpec((tile, LANES), lambda i: (first + i, 0)),
            pl.BlockSpec((tile, LANES), lambda i: (first + i, 0)),
            pl.BlockSpec((count, LANES), lambda i: (0, 0), **fixed),
            pl.BlockSpec((count, LANES), lambda i: (0, 0), **fixed),
            pl.BlockSpec((tile, 1), lambda i: (first + i, 0)),
            pl.BlockSpec((1, count), lambda i: (0, 0), **fixed),
        ]
        + [pl.BlockSpec(memory_space=pl.ANY)] * len(earlier),
        out_specs=[
            pl.BlockSpec((tile, width), lambda i: (i, 0)),
            pl.BlockSpec((tile, width), lambda i: (first + i, 0)),
            pl.BlockSpec((heads, tile), lambda i: (0, first + i)),
        ],
        out_shape=[
            jax.ShapeDtypeStruct((rows, width), jnp.bfloat16),
            jax.ShapeDtypeStruct((count, width), jnp.bfloat16),
            jax.ShapeDtypeStruct((heads, count), jnp.float32),
        ],
        input_output_aliases={9 + at: 1 + at for at in range(len(earlier))},
        scratch_shapes=[pltpu.VMEM((count, width), jnp.bfloat16), pltpu.VMEM((count, width), jnp.bfloat16)],
        compiler_params=pltpu.CompilerParams(vmem_limit_bytes=VMEM_BYTES),
        cost_estimate=pl.CostEstimate(
            flops=8 * rows * count * width,
            bytes_accessed=4 * count * width * 3 + 2 * rows * width,
            transcendentals=rows * count * heads,
        ),
        name="attend",
    )(projected, projected, projected, *tables, *tables, seg_col, seg_row, *earlier)


def attend_back_kernel(
    query_ref, key_ref, value_ref, cos_tile, sin_tile, cos_ref, sin_ref, seg_col, seg_row,
    upstream_ref, context_ref, total_ref, query_out, key_out, value_out, keys, values, key_grad, value_grad, *, first
):
    score_scale = HD ** (-0.5)
    pair, step = first + pl.program_id(0), pl.program_id(1)

    @pl.when(step == 0)
    def _():
        keys[...] = rotate(key_ref[...], cos_ref[...], sin_ref[...]).astype(jnp.bfloat16)
        values[...] = value_ref[...].astype(jnp.bfloat16)
        key_grad[...] = jnp.zeros_like(key_grad)
        value_grad[...] = jnp.zeros_like(value_grad)

    rows = query_ref.shape[0]
    lane = lane_of(rows)
    allowed = seg_col[...] == seg_row[...]
    query = rotate(query_ref[...], cos_tile[...], sin_tile[...]) * score_scale
    upstream = upstream_ref[...].astype(jnp.float32)
    product = upstream * context_ref[...].astype(jnp.float32)
    query_grad = jnp.zeros((rows, LANES), jnp.float32)
    for half in range(2):
        own = lane // HD == half
        own_query = jnp.where(own, query, 0.0).astype(jnp.bfloat16)
        own_upstream = jnp.where(own, upstream, 0.0).astype(jnp.bfloat16)
        picks = (lane_of(8) // HD == half).astype(jnp.float32)
        delta = contract(picks, product, 1, 1, precision=lax.Precision.HIGHEST)[0:1]
        total = total_ref[pl.ds(2 * pair + half, 1), :]
        scores = contract(keys[...], own_query, 1, 1)
        probs = jnp.where(allowed, jnp.exp(scores - total), 0.0)
        prob_grad = contract(values[...], own_upstream, 1, 1)
        score_grad = (probs * (prob_grad - delta)).astype(jnp.bfloat16)
        value_grad[...] += contract(probs.astype(jnp.bfloat16), own_upstream, 1, 0)
        key_grad[...] += contract(score_grad, own_query, 1, 0)
        spread = contract(score_grad, keys[...], 0, 0)
        query_grad = jnp.where(own, spread, query_grad)
    query_out[...] = unrotate(query_grad * score_scale, cos_tile[...], sin_tile[...]).astype(jnp.bfloat16)

    @pl.when(step == pl.num_programs(1) - 1)
    def _():
        key_out[...] = unrotate(key_grad[...], cos_ref[...], sin_ref[...]).astype(jnp.bfloat16)
        value_out[...] = value_grad[...].astype(jnp.bfloat16)


def attend_back(projected, tables, seg_col, seg_row, upstream, context, totals, first, taken, tile):
    count, width = projected.shape[0], projected.shape[1] // 3
    heads, pairs = width // HD, width // LANES
    fixed = dict(pipeline_mode=pl.Buffered(1))
    row_block = pl.BlockSpec((tile, LANES), lambda p, i: (i, first + p))
    whole_block = pl.BlockSpec((count, LANES), lambda p, i: (0, p))
    return pl.pallas_call(
        functools.partial(attend_back_kernel, first=first),
        grid=(taken, count // tile),
        in_specs=[
            row_block,
            pl.BlockSpec((count, LANES), lambda p, i: (0, pairs + first + p)),
            pl.BlockSpec((count, LANES), lambda p, i: (0, 2 * pairs + first + p)),
            pl.BlockSpec((tile, LANES), lambda p, i: (i, 0)),
            pl.BlockSpec((tile, LANES), lambda p, i: (i, 0)),
            pl.BlockSpec((count, LANES), lambda p, i: (0, 0), **fixed),
            pl.BlockSpec((count, LANES), lambda p, i: (0, 0), **fixed),
            pl.BlockSpec((count, 1), lambda p, i: (0, 0), **fixed),
            pl.BlockSpec((1, tile), lambda p, i: (0, i)),
            row_block,
            row_block,
            pl.BlockSpec((heads, tile), lambda p, i: (0, i)),
        ],
        out_specs=[pl.BlockSpec((tile, LANES), lambda p, i: (i, p)), whole_block, whole_block],
        out_shape=[jax.ShapeDtypeStruct((count, taken * LANES), jnp.bfloat16)] * 3,
        scratch_shapes=[
            pltpu.VMEM((count, LANES), jnp.bfloat16),
            pltpu.VMEM((count, LANES), jnp.bfloat16),
            pltpu.VMEM((count, LANES), jnp.float32),
            pltpu.VMEM((count, LANES), jnp.float32),
        ],
        compiler_params=pltpu.CompilerParams(vmem_limit_bytes=VMEM_BYTES),
        cost_estimate=pl.CostEstimate(
            flops=20 * count * count * taken * LANES,
            bytes_accessed=22 * count * taken * LANES,
            transcendentals=2 * count * count * taken,
        ),
        name="attend_back",
    )(projected, projected, projected, *tables, *tables, seg_col, seg_row, upstream, context, totals)


def feed_kernel(
    tokens_ref, own_ref, other_ref, cot_ref, gain_ref, gate_w, up_w, down_w,
    *refs,
):
    hidden_ref, turned_ref, acts_ref, out_ref, grad_ref, gain_grad_ref = refs[-6:]
    middle = tokens_ref[...].astype(jnp.float32) + (
        own_ref[...].astype(jnp.float32) + other_ref[...].astype(jnp.float32)
    )
    center = middle - jnp.mean(middle, axis=-1, keepdims=True)
    normed = center * lax.rsqrt(jnp.mean(center * center, axis=-1, keepdims=True) + EPSILON)
    hidden = (normed * gain_ref[...]).astype(jnp.bfloat16)
    hidden_ref[...] = hidden.T
    turned_ref[...] = cot_ref[...].T
    gate = contract(hidden, gate_w[...], 1, 0)
    upward = contract(hidden, up_w[...], 1, 0)
    mixed_grad = contract(cot_ref[...], down_w[...], 1, 0)
    share = 0.5 * (1.0 + lax.erf(gate * 0.7071067811865476))
    active = gate * share
    slope = share + gate * jnp.exp(-0.5 * gate * gate) * 0.3989422804014327
    size = gate.shape[1]
    gate_grad = (mixed_grad * upward * slope).astype(jnp.bfloat16)
    up_grad = (mixed_grad * active).astype(jnp.bfloat16)
    mixed = (active * upward).astype(jnp.bfloat16)
    acts_ref[:, :size] = gate_grad
    acts_ref[:, size : 2 * size] = up_grad
    acts_ref[:, 2 * size :] = mixed
    out_ref[...] = contract(mixed, down_w[...], 1, 1).astype(jnp.bfloat16)
    partial = contract(gate_grad, gate_w[...], 1, 1) + contract(up_grad, up_w[...], 1, 1)
    grad_ref[...] = partial.astype(jnp.bfloat16)

    @pl.when(pl.program_id(0) == 0)
    def _():
        gain_grad_ref[...] = jnp.zeros_like(gain_grad_ref)

    gain_grad_ref[...] += jnp.sum(partial * normed, axis=0, keepdims=True)


def feed(tokens, own, other, cotangent, gain, ffn_full, start, tile, earlier=()):
    rows, model = own.shape
    size = ffn_full.shape[1] // 3
    first = start // tile
    fixed = dict(pipeline_mode=pl.Buffered(1))
    row_block = pl.BlockSpec((tile, model), lambda i: (i, 0))
    late_block = pl.BlockSpec((tile, model), lambda i: (first + i, 0))
    return pl.pallas_call(
        feed_kernel,
        grid=(rows // tile,),
        in_specs=[
            late_block, row_block, row_block, late_block,
            pl.BlockSpec((1, model), lambda i: (0, 0), **fixed),
            pl.BlockSpec((model, size), lambda i: (0, 0), **fixed),
            pl.BlockSpec((model, size), lambda i: (0, 1), **fixed),
            pl.BlockSpec((model, size), lambda i: (0, 2), **fixed),
        ]
        + [pl.BlockSpec(memory_space=pl.ANY)] * len(earlier),
        out_specs=[
            pl.BlockSpec((model, tile), lambda i: (0, first + i)),
            pl.BlockSpec((model, tile), lambda i: (0, first + i)),
            pl.BlockSpec((tile, 3 * size), lambda i: (first + i, 0)),
            row_block, row_block,
            pl.BlockSpec((1, model), lambda i: (0, 0)),
        ],
        out_shape=[
            jax.ShapeDtypeStruct((model, tokens.shape[0]), jnp.bfloat16),
            jax.ShapeDtypeStruct((model, tokens.shape[0]), jnp.bfloat16),
            jax.ShapeDtypeStruct((tokens.shape[0], 3 * size), jnp.bfloat16),
            jax.ShapeDtypeStruct((rows, model), jnp.bfloat16),
            jax.ShapeDtypeStruct((rows, model), jnp.bfloat16),
            jax.ShapeDtypeStruct((1, model), jnp.float32),
        ],
        input_output_aliases={8 + at: at for at in range(len(earlier))},
        compiler_params=pltpu.CompilerParams(vmem_limit_bytes=VMEM_BYTES),
        cost_estimate=pl.CostEstimate(
            flops=12 * rows * model * size,
            bytes_accessed=2 * (3 * model * size + 7 * rows * model + 3 * rows * size),
            transcendentals=2 * rows * size,
        ),
        name="feed",
    )(tokens, own, other, cotangent, gain, ffn_full, ffn_full, ffn_full, *earlier)


def norm_of(values):
    center = values - jnp.mean(values, axis=-1, keepdims=True)
    inverse = lax.rsqrt(jnp.mean(center * center, axis=-1, keepdims=True) + EPSILON)
    return center * inverse, inverse


def norm_back(gradient, normed, inverse, gain):
    scaled = gradient * gain
    return inverse * (
        scaled
        - jnp.mean(scaled, axis=-1, keepdims=True)
        - normed * jnp.mean(scaled * normed, axis=-1, keepdims=True)
    )


def project_kernel(count, places_ref, tokens_ref, *refs):
    pieces = refs[:count]
    hidden_ref, projected_ref, weight_ref, out_ref, gain_ref, columns = refs[count:]
    rows, width, total = pieces[0].shape[0], weight_ref.shape[1], weight_ref.shape[1] + out_ref.shape[1]

    @pl.when(pl.program_id(0) == 0)
    def _():
        for index, piece in enumerate(pieces):
            at = pl.ds(pl.multiple_of(places_ref[index] * rows, rows), rows)
            weight_ref[at, :] = piece[:, :width]
            out_ref[at, :] = piece[:, width:total]
            columns[at, :] = piece[:, total:].astype(jnp.float32)
        gain_ref[...] = columns[...].T[: gain_ref.shape[0]]

    normed, _ = norm_of(tokens_ref[...].astype(jnp.float32))
    hidden = (normed * gain_ref[0:1]).astype(jnp.bfloat16)
    hidden_ref[...] = hidden
    projected_ref[...] = contract(hidden, weight_ref[...], 1, 0)


def project(tokens, pieces, places, tile):
    (count, model), joined = tokens.shape, pieces[0].shape[1] - LANES
    width = joined // 4 * 3
    fixed = dict(pipeline_mode=pl.Buffered(1))
    return pl.pallas_call(
        functools.partial(project_kernel, len(pieces)),
        grid=(count // tile,),
        in_specs=[pl.BlockSpec(memory_space=pltpu.SMEM), pl.BlockSpec((tile, model), lambda i: (i, 0))]
        + [pl.BlockSpec(piece.shape, lambda i: (0, 0), **fixed) for piece in pieces],
        out_specs=[
            pl.BlockSpec((tile, model), lambda i: (i, 0)),
            pl.BlockSpec((tile, width), lambda i: (i, 0)),
            pl.BlockSpec((model, width), lambda i: (0, 0)),
            pl.BlockSpec((model, joined - width), lambda i: (0, 0)),
            pl.BlockSpec((8, model), lambda i: (0, 0)),
        ],
        out_shape=[
            jax.ShapeDtypeStruct((count, model), jnp.bfloat16),
            jax.ShapeDtypeStruct((count, width), jnp.float32),
            jax.ShapeDtypeStruct((model, width), jnp.bfloat16),
            jax.ShapeDtypeStruct((model, joined - width), jnp.bfloat16),
            jax.ShapeDtypeStruct((8, model), jnp.float32),
        ],
        scratch_shapes=[pltpu.VMEM((model, LANES), jnp.float32)],
        compiler_params=pltpu.CompilerParams(vmem_limit_bytes=VMEM_BYTES),
        cost_estimate=pl.CostEstimate(
            flops=2 * count * model * width,
            bytes_accessed=4 * count * model + 4 * count * width + 4 * model * width,
            transcendentals=0,
        ),
        name="project",
    )(places, tokens, *pieces)


def project_back_kernel(groups, tokens_ref, weight_ref, *refs):
    grads, (out_ref, gain_grad_ref) = refs[: 3 * groups], refs[3 * groups :]
    size = grads[0].shape[1]
    partial = 0.0
    for at, ref in enumerate(grads):
        begin = (at % 3 * groups + at // 3) * size
        partial = partial + contract(ref[...], weight_ref[:, begin : begin + size], 1, 1)
    out_ref[...] = partial.astype(jnp.bfloat16)
    normed, _ = norm_of(tokens_ref[...].astype(jnp.float32))

    @pl.when(pl.program_id(0) == 0)
    def _():
        gain_grad_ref[...] = jnp.zeros_like(gain_grad_ref)

    gain_grad_ref[...] += jnp.sum(partial * normed, axis=0, keepdims=True)


def project_back(tokens, grads, weight, start, rows, tile):
    model, first = tokens.shape[1], start // tile
    late = lambda i: (first + i, 0)
    return pl.pallas_call(
        functools.partial(project_back_kernel, len(grads) // 3),
        grid=(rows // tile,),
        in_specs=[
            pl.BlockSpec((tile, model), late),
            pl.BlockSpec(weight.shape, lambda i: (0, 0), pipeline_mode=pl.Buffered(1)),
        ]
        + [pl.BlockSpec((tile, grad.shape[1]), late) for grad in grads],
        out_specs=[pl.BlockSpec((tile, model), lambda i: (i, 0)), pl.BlockSpec((1, model), lambda i: (0, 0))],
        out_shape=[jax.ShapeDtypeStruct((rows, model), jnp.bfloat16), jax.ShapeDtypeStruct((1, model), jnp.float32)],
        compiler_params=pltpu.CompilerParams(vmem_limit_bytes=VMEM_BYTES),
        cost_estimate=pl.CostEstimate(
            flops=2 * rows * model * weight.shape[1],
            bytes_accessed=4 * rows * model + 2 * (rows + model) * weight.shape[1],
            transcendentals=0,
        ),
        name="project_back",
    )(tokens, weight, *grads)


def parted_weights_kernel(core_ref, hidden_ref, gradient_ref, *refs):
    rights, outs = refs[:4], refs[4:]
    first_core = core_ref[0] == 0
    rows = hidden_ref.shape[1] // 4
    width = rights[0].shape[1]
    for index, right in enumerate(rights):
        left_ref = gradient_ref if index == 3 else hidden_ref
        product = contract(left_ref[...], right[...], 0, 0).astype(jnp.bfloat16)
        kept_ref, sent_ref = outs[index // 2 * 2 : index // 2 * 2 + 2]
        cols = slice(index % 2 * width, (index % 2 + 1) * width)
        for pair in range(2):
            even = product[2 * pair * rows : (2 * pair + 1) * rows]
            odd = product[(2 * pair + 1) * rows : (2 * pair + 2) * rows]
            at = slice(pair * rows, (pair + 1) * rows)
            kept_ref[at, cols] = jnp.where(first_core, even, odd)
            sent_ref[at, cols] = jnp.where(first_core, odd, even)


def parted_weights(hidden, gradient, rights, core, outers):
    count, model = hidden.shape
    width = rights[0].shape[1]
    tile = model // outers
    half_block = pl.BlockSpec((tile // 2, 2 * width), lambda i: (i, 0))
    left_block = pl.BlockSpec((count, tile), lambda i: (0, i))
    return pl.pallas_call(
        parted_weights_kernel,
        grid=(outers,),
        in_specs=[pl.BlockSpec(memory_space=pltpu.SMEM), left_block, left_block]
        + [pl.BlockSpec(right.shape, lambda i: (0, 0), pipeline_mode=pl.Buffered(1)) for right in rights],
        out_specs=[half_block] * 4,
        out_shape=[jax.ShapeDtypeStruct((model // 2, 2 * width), jnp.bfloat16)] * 4,
        compiler_params=pltpu.CompilerParams(vmem_limit_bytes=VMEM_BYTES),
        cost_estimate=pl.CostEstimate(
            flops=8 * count * model * width, bytes_accessed=8 * (count + model) * width + 4 * count * model,
            transcendentals=0,
        ),
        name="parted_weights",
    )(core, hidden, gradient, *rights)


def middle_back_kernel(
    tokens_ref, own_ref, other_ref, own_grad_ref, other_grad_ref, cot_ref, gain_ref, out_w, *refs
):
    grad_ref, context_grad_ref = refs[-2:]
    middle = tokens_ref[...].astype(jnp.float32) + (
        own_ref[...].astype(jnp.float32) + other_ref[...].astype(jnp.float32)
    )
    normed, inverse = norm_of(middle)
    gradient = own_grad_ref[...].astype(jnp.float32) + other_grad_ref[...].astype(jnp.float32)
    back = norm_back(gradient, normed, inverse, gain_ref[...])
    gradient = (cot_ref[...].astype(jnp.float32) + back).astype(jnp.bfloat16)
    grad_ref[...] = gradient
    context_grad_ref[...] = contract(gradient, out_w[...], 1, 0).astype(jnp.bfloat16)


def middle_back(tokens, own, other, own_grad, other_grad, cotangent, gain, out_w, start, tile, earlier=()):
    rows, model = own.shape
    width, first = out_w.shape[1], start // tile
    row_block = pl.BlockSpec((tile, model), lambda i: (i, 0))
    late_block = pl.BlockSpec((tile, model), lambda i: (first + i, 0))
    return pl.pallas_call(
        middle_back_kernel,
        grid=(rows // tile,),
        in_specs=[
            late_block, row_block, row_block, row_block, row_block, late_block,
            pl.BlockSpec((1, model), lambda i: (0, 0)),
            pl.BlockSpec((model, width), lambda i: (0, 0), pipeline_mode=pl.Buffered(1)),
        ]
        + [pl.BlockSpec(memory_space=pl.ANY)] * len(earlier),
        out_specs=[late_block, pl.BlockSpec((tile, width), lambda i: (first + i, 0))],
        out_shape=[
            jax.ShapeDtypeStruct(tokens.shape, jnp.bfloat16),
            jax.ShapeDtypeStruct((tokens.shape[0], width), jnp.bfloat16),
        ],
        input_output_aliases={8 + at: at for at in range(len(earlier))},
        compiler_params=pltpu.CompilerParams(vmem_limit_bytes=VMEM_BYTES),
        cost_estimate=pl.CostEstimate(
            flops=2 * rows * model * width, bytes_accessed=2 * (7 * rows * model + model * width), transcendentals=0
        ),
        name="middle_back",
    )(tokens, own, other, own_grad, other_grad, cotangent, gain, out_w, *earlier)


def last_kernel(tokens_ref, own_grad_ref, other_grad_ref, above_ref, gain_ref, grad_ref):
    normed, inverse = norm_of(tokens_ref[...].astype(jnp.float32))
    gradient = own_grad_ref[...].astype(jnp.float32) + other_grad_ref[...].astype(jnp.float32)
    grad_ref[...] = above_ref[...].astype(jnp.float32) + norm_back(gradient, normed, inverse, gain_ref[...])


def last(tokens, own_grad, other_grad, above, gain, start, tile, earlier=()):
    rows, model = own_grad.shape
    first = start // tile
    row_block = pl.BlockSpec((tile, model), lambda i: (i, 0))
    late_block = pl.BlockSpec((tile, model), lambda i: (first + i, 0))

    def body(*refs):
        last_kernel(*refs[:5], refs[-1])

    return pl.pallas_call(
        body,
        grid=(rows // tile,),
        in_specs=[late_block, row_block, row_block, late_block, pl.BlockSpec((1, model), lambda i: (0, 0))]
        + [pl.BlockSpec(memory_space=pl.ANY)] * len(earlier),
        out_specs=late_block,
        out_shape=jax.ShapeDtypeStruct(tokens.shape, jnp.float32),
        input_output_aliases={5 + at: at for at in range(len(earlier))},
        compiler_params=pltpu.CompilerParams(vmem_limit_bytes=VMEM_BYTES),
        cost_estimate=pl.CostEstimate(flops=20 * rows * model, bytes_accessed=12 * rows * model, transcendentals=0),
        name="last",
    )(tokens, own_grad, other_grad, above, gain, *earlier)


def feed_weights_kernel(hidden_ref, cot_ref, acts_ref, out_ref):
    @pl.when(pl.program_id(0) < 2)
    def _():
        out_ref[...] = contract(hidden_ref[...], acts_ref[...], 1, 0).astype(jnp.bfloat16)

    @pl.when(pl.program_id(0) == 2)
    def _():
        out_ref[...] = contract(cot_ref[...], acts_ref[...], 1, 0).astype(jnp.bfloat16)


def feed_weights(hidden, cotangent, acts, tile):
    model, count = hidden.shape
    size = acts.shape[1] // 3
    return pl.pallas_call(
        feed_weights_kernel,
        grid=(3, model // tile),
        in_specs=[
            pl.BlockSpec((tile, count), lambda j, i: (i, 0)),
            pl.BlockSpec((tile, count), lambda j, i: (i, 0)),
            pl.BlockSpec((count, size), lambda j, i: (0, j)),
        ],
        out_specs=pl.BlockSpec((tile, size), lambda j, i: (i, j)),
        out_shape=jax.ShapeDtypeStruct((model, 3 * size), jnp.bfloat16),
        compiler_params=pltpu.CompilerParams(vmem_limit_bytes=VMEM_BYTES),
        cost_estimate=pl.CostEstimate(
            flops=6 * count * model * size, bytes_accessed=6 * count * size + 4 * count * model + 6 * model * size,
            transcendentals=0,
        ),
        name="feed_weights",
    )(hidden, cotangent, acts)


def positions(segment_ids):
    index_row = jnp.arange(segment_ids.shape[0], dtype=jnp.int32)
    change = jnp.concatenate([jnp.ones((1,), bool), segment_ids[1:] != segment_ids[:-1]])
    marker = jnp.where(change, index_row, jnp.zeros_like(index_row))
    starts = lax.cummax(marker, axis=0)
    return (index_row - starts).astype(jnp.float32)


def rope_tables(places):
    half = HD // 2
    inverse = ROPE_BASE ** (-2.0 * jnp.arange(half, dtype=jnp.float32) / HD)
    angles = places[:, None] * inverse[None, :]
    cosine, sine = jnp.cos(angles), jnp.sin(angles)
    return (
        jnp.concatenate([cosine] * 4, axis=1),
        jnp.concatenate([-sine, sine, -sine, sine], axis=1),
    )


def shifted(count, inner, step):
    return [(a * inner + b, (a + step) % count * inner + b) for a in range(count) for b in range(inner)]


def flipped(count, bit):
    return [(i, i ^ bit) for i in range(count)]


def place_of(count):
    here = lax.axis_index("dp")
    return here // 4, (here // 2) % 2, here % 2, count // 4


def gather_pieces(shard, ahead):
    count = lax.axis_size("dp")
    if count % 4:
        return [lax.all_gather(shard, "dp", axis=0, tiled=True)], jnp.zeros((1,), jnp.int32), shard, ahead
    outer, pair, core, outers = place_of(count)
    pieces = [(shard, outer, pair)]
    for back in range(1, outers):
        moved = lax.ppermute(shard, "dp", shifted(outers, 4, back))
        pieces.append((moved, (outer - back) % outers, pair))
    for at, (piece, outer_at, _) in enumerate(list(pieces)):
        if at == 1:
            piece, ahead = lax.optimization_barrier((piece, ahead))
            early = pieces[-1][0]
        pieces.append((lax.ppermute(piece, "dp", flipped(count, 2)), outer_at, 1 - pair))
    found, places = [], []
    for piece, outer_at, pair_at in pieces:
        found += [piece, lax.ppermute(piece, "dp", flipped(count, 1))]
        chip = (outer_at * 2 + pair_at) * 2
        places += [chip + core, chip + 1 - core]
    return found, jnp.stack(places).astype(jnp.int32), early, ahead


def scatter_rows(kept, sent):
    count = lax.axis_size("dp")
    outer, pair, _, outers = place_of(count)
    got = lax.ppermute(sent, "dp", flipped(count, 1))
    rows = 2 * kept.shape[0] // count
    kept, got = (values.reshape(outers, 2, rows, -1) for values in (kept, got))

    def total_at(kept, got, at, axis):
        pick = lambda values: lax.dynamic_index_in_dim(values, at, axis, keepdims=False).astype(jnp.float32)
        return pick(kept) + pick(got)

    sent = total_at(kept, got, 1 - pair, 1).astype(jnp.bfloat16)
    kept = total_at(kept, got, pair, 1).astype(jnp.bfloat16)
    got = lax.ppermute(sent, "dp", flipped(count, 2))
    total = total_at(kept, got, outer, 0)
    moved = []
    for step in range(1, outers):
        sent = total_at(kept, got, (outer + step) % outers, 0).astype(jnp.bfloat16)
        moved.append(lax.ppermute(sent, "dp", shifted(outers, 4, step)))
    return total + sum(values.astype(jnp.float32) for values in moved), got


def scatter_weights(hidden, gradient, rights):
    count, width = lax.axis_size("dp"), rights[0].shape[1]
    if count % 4:
        lefts = (hidden, hidden, hidden, gradient)
        partial = [contract(left, right, 0, 0) for left, right in zip(lefts, rights)]
        partial = jnp.concatenate(partial, axis=1).astype(jnp.bfloat16)
        total = lax.psum_scatter(partial, "dp", scatter_dimension=0, tiled=True).astype(jnp.float32)
        return [total[:, at * width : (at + 1) * width] for at in range(4)], total
    _, _, core, outers = place_of(count)
    halves = parted_weights(hidden, gradient, rights, core.astype(jnp.int32)[None], outers)
    total_a, late = scatter_rows(*halves[:2])
    total_b, _ = scatter_rows(*halves[2:])
    return [total[:, at * width : (at + 1) * width] for total in (total_a, total_b) for at in range(2)], late


def whole_sum(values, mp_size, after):
    count = lax.axis_size("dp")
    if count % 4 or mp_size != 2:
        return lax.psum(values, ("dp", "mp"))
    other = lax.ppermute(values, "mp", [(0, 1), (1, 0)])
    other, _ = lax.optimization_barrier((other, after))
    values = values + other
    values = values + lax.ppermute(values, "dp", flipped(count, 1))
    values = values + lax.ppermute(values, "dp", flipped(count, 2))
    moved = [lax.ppermute(values, "dp", shifted(count // 4, 4, step)) for step in range(1, count // 4)]
    return values + sum(moved)


def from_pair(rounded):
    if lax.axis_size("mp") != 2:
        total = lax.psum(rounded, "mp").astype(jnp.float32) - rounded.astype(jnp.float32)
        return total.astype(rounded.dtype)
    return lax.ppermute(rounded, "mp", [(0, 1), (1, 0)])


def layer(tokens, segment_ids, attn_gain, w_qkv, w_out, mlp_gain, w_in, w_ff_out, cotangent):
    count, _ = tokens.shape
    shard_rows, width, hidden_here = w_qkv.shape[0], w_qkv.shape[2], w_in.shape[2]
    spare = -hidden_here % LANES
    size = hidden_here + spare
    tile = count // 4
    chunks = ((0, 2 * tile), (2 * tile, 2 * tile))
    late_chunks = ((0, tile), (tile, 2 * tile), (3 * tile, tile))

    def padded(values):
        return jnp.pad(values, ((0, 0), (0, spare)))

    gains = jnp.pad(jnp.stack([attn_gain, mlp_gain], axis=1), ((0, 0), (0, LANES - 2)))
    tables = rope_tables(positions(segment_ids))
    first_shard = jnp.concatenate([w_qkv.reshape(shard_rows, -1), w_out.T, gains], axis=1)
    pieces, places, early, tables = gather_pieces(first_shard, tables)
    ffn_shard = jnp.concatenate([padded(w_in[:, 0]), padded(w_in[:, 1]), padded(w_ff_out.T)], axis=1)
    ffn_shard, _ = lax.optimization_barrier((ffn_shard, early))
    ffn_full = lax.all_gather(ffn_shard, "dp", axis=0, tiled=True)
    seg_col, seg_row = segment_ids[:, None], segment_ids[None, :]
    hidden_one, projected, qkv_w, out_w, gain_rows = project(tokens, pieces, places, tile)
    gain_one, gain_two = gain_rows[0:1], gain_rows[1:2]

    kept, own, other = (), [], []
    for start, rows in chunks:
        part, *kept = attend(projected, tables, seg_col, seg_row, start, rows, tile, kept)
        partial = contract(part, out_w, 1, 1).astype(jnp.bfloat16)
        own.append(partial)
        other.append(from_pair(partial))
    context, totals = kept

    kept, outs, grads, other_grads, gain_two_grad = (), [], [], [], 0.0
    for at, (start, rows) in enumerate(chunks):
        *kept, out, grad, gain_grad = feed(tokens, own[at], other[at], cotangent, gain_two, ffn_full, start, tile, kept)
        outs.append(out)
        grads.append(grad)
        other_grads.append(from_pair(grad))
        gain_two_grad = gain_two_grad + gain_grad
    feed_grads = feed_weights(*kept, tile)
    ffn_total = lax.psum_scatter(feed_grads, "dp", scatter_dimension=0, tiled=True).astype(jnp.float32)

    kept = ()
    for at, (start, rows) in enumerate(chunks):
        kept = middle_back(
            tokens, own[at], other[at], grads[at], other_grads[at], cotangent, gain_two, out_w, start, tile, kept
        )
    attn_grad_in, context_grad = kept
    outs, _ = lax.optimization_barrier((outs, other_grads[-1]))
    other_outs = []
    for out in outs:
        other_outs.append(from_pair(out))

    qkv_grads = attend_back(
        projected, tables, seg_col, seg_row, context_grad, context, totals, 0, width // LANES, count
    )
    totals, late = scatter_weights(hidden_one, attn_grad_in, [*qkv_grads, context])
    query_total, key_total, value_total, out_total = totals
    one_own, one_other, gain_one_grad = [], [], 0.0
    for start, rows in late_chunks:
        partial, gain_grad = project_back(tokens, qkv_grads, qkv_w, start, rows, tile)
        gain_one_grad = gain_one_grad + gain_grad
        one_own.append(partial)
        one_other.append(from_pair(partial))
    gain_total = whole_sum(jnp.concatenate([gain_one_grad, gain_two_grad]), lax.axis_size("mp"), late)
    gain_total = lax.dynamic_slice_in_dim(gain_total, lax.axis_index("dp") * shard_rows, shard_rows, axis=1)
    input_grad = ()
    for at, (start, _) in enumerate(late_chunks):
        input_grad = (
            last(tokens, one_own[at], one_other[at], attn_grad_in, gain_one, start, tile, input_grad),
        )
    output = jnp.concatenate(
        [
            (
                tokens[start : start + rows].astype(jnp.float32)
                + own[at].astype(jnp.float32)
                + other[at].astype(jnp.float32)
                + outs[at].astype(jnp.float32)
                + other_outs[at].astype(jnp.float32)
            ).astype(jnp.bfloat16)
            for at, (start, rows) in enumerate(chunks)
        ]
    )
    return (
        output,
        input_grad[0],
        gain_total[0],
        jnp.stack([query_total, key_total, value_total], axis=1),
        out_total.T,
        gain_total[1],
        jnp.stack([ffn_total[:, :hidden_here], ffn_total[:, size : size + hidden_here]], axis=1),
        ffn_total[:, 2 * size : 2 * size + hidden_here].T,
    )


def solution(mesh):
    return jax.shard_map(
        layer,
        mesh=mesh,
        in_specs=(
            P("dp", None),
            P("dp"),
            P("dp"),
            P("dp", None, "mp"),
            P("mp", "dp"),
            P("dp"),
            P("dp", None, "mp"),
            P("mp", "dp"),
            P("dp", None),
        ),
        out_specs=(
            P("dp", None),
            P("dp", None),
            P("dp"),
            P("dp", None, "mp"),
            P("mp", "dp"),
            P("dp"),
            P("dp", None, "mp"),
            P("mp", "dp"),
        ),
        check_vma=False,
    )
```
